128 devices in a mesh: dp: 16 (over z, x), member: 8 (over y, core).
Axes of the slice: x: 4, y: 4, z: 4, core: 2. Of those that a mesh axis runs over, the one named last changes fastest.
Arguments:
- fixed_rows: bfloat16 [131072, 2048], P(('dp', 'member')), may hold values from -600 to 600
- member_rows: bfloat16 [131072, 256], P(('dp', 'member')), may hold values from -0.375 to 0.375
- target: float32 [131072], P(('dp', 'member')), may hold values from -6 to 6
- fixed_prev: bfloat16 [2048], replicated, may hold values from -0.59765625 to 0.59765625
- member_id: int32 [131072], P(('dp', 'member')), may hold values from 0 to 511, as said below
Outputs:
- fixed_coef: float32 [2048], replicated
- member_coef: float32 [512, 256], P(('dp', 'member'))
- row_scores: float32 [131072], P(('dp', 'member'))
The draws below stay inside these ranges and needn't reach their ends.
Inputs may be any that keep to these rules, and one draw needn't show every extreme that they name: `member_id`: member m belongs to owner m // 4, the device of that index along dp+member, which holds its row of member_coef. Among the 1024 rows of one device (aligned blocks) at most 24 have members of one owner; in every draw one owner gets exactly 24 rows from every device.
All inputs are finite; a program needn't handle non-finite values.
Results may differ from the reference program's by a relative error of at most 0.006.
Values may be sent and summed in bfloat16 or wider, within the bound.
No kernel may reach another device: no remote copies, remote signals or barrier semaphores. Data moves between devices by JAX's collectives and lax.ppermute only.
A program may use at most 192 MiB of HBM per device.

```python
import math
import jax
import jax.numpy as jnp
from jax import lax

FIX = 2048
MEM = 256
ROW_DEV = 1024
MEM_DEV = 4
CAP = 24
ROWS = 131072
MEMBERS = 512
DEVICES = 128


def draw_member_id(key, part):
    devices = ROWS // ROW_DEV
    slot_total = devices * CAP
    favored = jax.random.randint(jax.random.fold_in(key, 7), (), 0, devices)

    def one_device(dev_key):
        key_rank, key_order, key_member = jax.random.split(dev_key, 3)
        slot_ids = jnp.arange(slot_total, dtype=jnp.int32)
        rank_list = jax.random.permutation(key_rank, slot_total).astype(jnp.int32)
        slot_rank = jnp.where(slot_ids // CAP == favored, slot_ids % CAP - CAP, rank_list)
        chosen = jnp.argsort(slot_rank, stable=True)[:ROW_DEV].astype(jnp.int32)
        chosen = chosen[jax.random.permutation(key_order, ROW_DEV)]
        owners = chosen // CAP
        return owners * MEM_DEV + jax.random.randint(key_member, (ROW_DEV,), 0, MEM_DEV)
    device_keys = jax.random.split(jax.random.fold_in(key, 11), devices)
    return jax.vmap(one_device)(device_keys).reshape(ROWS).astype(jnp.int32)


def draw_fixed_rows(key, part):
    devices = ROWS // ROW_DEV
    band = FIX // devices
    key_perm, key_rho, key_scale, key_pair, key_rows = jax.random.split(jax.random.fold_in(key, 23), 5)
    partner = jax.random.permutation(key_perm, FIX).astype(jnp.int32)
    decay = jax.random.uniform(key_rho, (FIX,), jnp.float32, 0.94, 0.995)
    col_scale = jnp.exp(jax.random.uniform(key_scale, (FIX,), jnp.float32, math.log(0.1), 0.0))
    pairing = jax.random.permutation(key_pair, devices).astype(jnp.int32)
    col_block = jnp.arange(FIX, dtype=jnp.int32) // band
    level = math.sqrt(8192.0 / ROWS)

    def one_block(dev):
        block_key = jax.random.fold_in(key_rows, dev)
        key_noise = jax.random.fold_in(block_key, 0)
        noise = jnp.clip(jax.random.normal(key_noise, (ROW_DEV, FIX), jnp.float32), -4.5, 4.5)
        mixed = noise - decay[None, :] * noise[:, partner]
        spike = jnp.where(col_block == pairing[dev], 6.0, 1.0)
        return (level * col_scale[None, :] * spike[None, :] * mixed).astype(jnp.bfloat16)
    blocks = lax.map(one_block, jnp.arange(devices, dtype=jnp.int32))
    return blocks.reshape(ROWS, FIX)


def levels(stream_key, shape, pieces, least, largest):
    level, own = 1.0, jax.random.fold_in(stream_key, 6)
    for dim, shards_of in pieces:
        steps = jnp.exp(jax.random.uniform(jax.random.fold_in(own, dim), (shards_of,), jnp.float32, least / len(pieces), largest / len(pieces)))
        level = level * jnp.repeat(steps, shape[dim] // shards_of).reshape([-1 if axis == dim else 1 for axis in range(len(shape))])
    return level


def scatter_about(stream_key, dims, spread, reach, cuts=(), kind=jnp.bfloat16):
    gain = levels(stream_key, dims, cuts, -0.22, 0.18) if cuts else 1.0
    entries = jax.random.normal(stream_key, dims, jnp.float32) * spread * gain
    return jnp.minimum(jnp.maximum(entries, -reach), reach).astype(kind)


def setup_inputs(seed: int = 0) -> dict:
    key_of = jax.random.split(jax.random.key(seed), 6)
    fixed_rows = draw_fixed_rows(jax.random.fold_in(key_of[5], 71), 0)
    member_rows = scatter_about(key_of[1], (ROWS, MEM), MEM ** -0.5, 0.375, ((0, 128),))
    target = scatter_about(key_of[2], (ROWS,), 1.0, 6.0, ((0, 128),), jnp.float32)
    fixed_prev = scatter_about(key_of[3], (FIX,), 0.1, 0.59765625)
    member_id = draw_member_id(jax.random.fold_in(key_of[5], 71), 0)
    return dict(fixed_rows=fixed_rows, member_rows=member_rows, target=target, fixed_prev=fixed_prev, member_id=member_id)


RIDGE_FIXED = 4.0
RIDGE_MEMBER = 1.0

def block_solve(matrix, right_side):
    order = matrix.shape[0]
    width = min(512, order)
    count = order // width
    hold = lax.Precision.HIGHEST
    eye_block = jnp.eye(width, dtype=jnp.float32)
    inverses = []
    panels = []
    work = matrix
    for step in range(count):
        lo = step * width
        hi = lo + width
        factor_blk = jnp.linalg.cholesky(work[lo:hi, lo:hi])
        inverse_blk = jax.scipy.linalg.solve_triangular(factor_blk, eye_block, lower=True)
        inverses.append(inverse_blk)
        if step + 1 < count:
            panel = jnp.dot(work[hi:, lo:hi], inverse_blk.T, precision=hold)
            panels.append(panel)
            work = work.at[hi:, hi:].add(-jnp.dot(panel, panel.T, precision=hold))
    forward = []
    for step in range(count):
        lo = step * width
        partial_rhs = right_side[lo:lo + width]
        for prior in range(step):
            lower_blk = panels[prior][(step - prior - 1) * width:(step - prior) * width]
            partial_rhs = partial_rhs - jnp.dot(lower_blk, forward[prior], precision=hold)
        forward.append(jnp.dot(inverses[step], partial_rhs, precision=hold))
    backward = [None] * count
    for step in range(count - 1, -1, -1):
        partial_rhs = forward[step]
        for later in range(step + 1, count):
            lower_blk = panels[step][(later - step - 1) * width:(later - step) * width]
            partial_rhs = partial_rhs - jnp.dot(lower_blk.T, backward[later], precision=hold)
        backward[step] = jnp.dot(inverses[step].T, partial_rhs, precision=hold)
    return jnp.concatenate(backward, axis=0)

def reference(fixed_rows, member_rows, target, fixed_prev, member_id):
    prior_score = jnp.dot(fixed_rows.astype(jnp.float32), fixed_prev.astype(jnp.float32), preferred_element_type=jnp.float32)
    member_resid = (target - prior_score).astype(jnp.bfloat16)
    owner_ids = (member_id // MEM_DEV).astype(jnp.int32)
    local_ids = (member_id % MEM_DEV).astype(jnp.int32)
    row_order = jnp.argsort(owner_ids, stable=True).astype(jnp.int32)
    counts = jnp.bincount(owner_ids, length=DEVICES).astype(jnp.int32)
    starts = (jnp.cumsum(counts) - counts).astype(jnp.int32)
    pad_width = DEVICES * CAP
    sorted_rows = jnp.concatenate([member_rows[row_order], jnp.zeros((pad_width, MEM), jnp.bfloat16)], axis=0)
    sorted_resid = jnp.concatenate([member_resid[row_order], jnp.zeros((pad_width,), jnp.bfloat16)], axis=0)
    sorted_local = jnp.concatenate([local_ids[row_order], jnp.full((pad_width,), -1, jnp.int32)], axis=0)
    identity_mem = jnp.eye(MEM, dtype=jnp.float32)

    def owner_solve(owner):
        first = starts[owner]
        block_rows = lax.dynamic_slice_in_dim(sorted_rows, first, pad_width, 0).astype(jnp.float32)
        block_resid = lax.dynamic_slice_in_dim(sorted_resid, first, pad_width, 0).astype(jnp.float32)
        block_local = lax.dynamic_slice_in_dim(sorted_local, first, pad_width, 0)
        is_valid = jnp.arange(pad_width, dtype=jnp.int32) < counts[owner]
        member_hot = ((block_local[:, None] == jnp.arange(MEM_DEV, dtype=jnp.int32)[None, :]) & is_valid[:, None]).astype(jnp.float32)
        weighted = member_hot[:, :, None] * block_rows[:, None, :]
        member_gram = jnp.einsum('smd,se->mde', weighted, block_rows, precision=lax.Precision.HIGHEST)
        member_rhs = jnp.einsum('sm,sd->md', member_hot * block_resid[:, None], block_rows, precision=lax.Precision.HIGHEST)
        return jax.vmap(block_solve)(member_gram + RIDGE_MEMBER * identity_mem, member_rhs)
    member_coef = lax.map(owner_solve, jnp.arange(DEVICES, dtype=jnp.int32)).reshape(MEMBERS, MEM)
    member_low = member_coef.astype(jnp.bfloat16)
    member_score = jnp.sum(member_rows.astype(jnp.float32) * member_low[member_id].astype(jnp.float32), axis=1)
    fixed_resid = (target - member_score).astype(jnp.bfloat16)

    def add_block(summed, block):
        block_f = block.astype(jnp.float32)
        return (summed + jnp.dot(block_f.T, block_f, precision=lax.Precision.HIGHEST), None)
    fixed_gram, unused = lax.scan(add_block, jnp.zeros((FIX, FIX), jnp.float32), fixed_rows.reshape(DEVICES, ROW_DEV, FIX))
    fixed_grad = jnp.dot(fixed_resid.astype(jnp.float32), fixed_rows.astype(jnp.float32), precision=lax.Precision.HIGHEST)
    fixed_coef = block_solve(fixed_gram + RIDGE_FIXED * jnp.eye(FIX, dtype=jnp.float32), fixed_grad)
    row_scores = jnp.dot(fixed_rows.astype(jnp.float32), fixed_coef.astype(jnp.bfloat16).astype(jnp.float32), preferred_element_type=jnp.float32) + member_score
    return (fixed_coef, member_coef, row_scores)
```

```python
import functools

import jax
import jax.numpy as jnp
from jax import lax
from jax.experimental import pallas as pl
from jax.experimental.pallas import tpu as pltpu
from jax.sharding import Mesh
from jax.sharding import PartitionSpec as P

F32 = jnp.float32
BF16 = jnp.bfloat16
HIGH = lax.Precision.HIGHEST
ALL = ("z", "x", "y", "core")
CHIPS = ("z", "x", "y")

MEM_DEV = 4
RIDGE_FIXED = 4.0
RIDGE_MEMBER = 1.0
GROUP = 1

FIX = 2048
MEM = 256
PAY = 384
BLK = 256
NBLK = FIX // BLK
CORE_PAIRS = 18


def pair_table():
    table = []
    for core in range(2):
        pairs = []
        for i in range(4 * core, 4 * core + 4):
            pairs += [(i, (i + k) % NBLK) for k in range(4)]
        pairs += [(0, 4), (1, 5)] if core == 0 else [(6, 2), (7, 3)]
        table.append([(max(p), min(p)) for p in pairs])
    return table


def params(mb=56):
    return pltpu.CompilerParams(vmem_limit_bytes=mb << 20)


def dot_nn(a, b, precision=None):
    return lax.dot_general(a, b, (((1,), (0,)), ((), ())), precision=precision, preferred_element_type=F32)


def dot_nt(a, b, precision=None):
    return lax.dot_general(a, b, (((1,), (1,)), ((), ())), precision=precision, preferred_element_type=F32)


def dot_tn(a, b, precision=None):
    return lax.dot_general(a, b, (((0,), (0,)), ((), ())), precision=precision, preferred_element_type=F32)


def split3(v):
    hi = v.astype(BF16)
    rest = v - hi.astype(F32)
    mid = rest.astype(BF16)
    low = (rest - mid.astype(F32)).astype(BF16)
    return hi, mid, low


def over_lanes(v, c):
    return jnp.broadcast_to(v[:, c : c + 1], v.shape)


def over_rows(v, i):
    return jnp.broadcast_to(v[i : i + 1, :], v.shape)


def factor128(blocks):
    n = len(blocks)
    sub = lax.broadcasted_iota(jnp.int32, (8, 128), 0)
    lane = lax.broadcasted_iota(jnp.int32, (8, 128), 1)
    a = [[blk[8 * t : 8 * t + 8, :] for t in range(16)] for blk in blocks]
    e = [[(lane == sub + 8 * t).astype(F32) for t in range(16)] for _ in blocks]
    out = [[] for _ in blocks]
    b = [[over_lanes(a[p][0], k) for k in range(8)] for p in range(n)]
    for s in range(16):
        more = s < 15
        r = [a[p][s] for p in range(n)]
        f = [e[p][s] for p in range(n)]
        if more:
            r1 = [a[p][s + 1] for p in range(n)]
            f1 = [e[p][s + 1] for p in range(n)]
            q = [[over_lanes(r1[p], 8 * s + k) for k in range(8)] for p in range(n)]
            bn = [[over_lanes(r1[p], 8 * s + 8 + k) for k in range(8)] for p in range(n)]
        scale = [jnp.zeros((8, 128), F32) for _ in range(n)]
        for i in range(8):
            for p in range(n):
                inv = 1.0 / over_rows(b[p][i], i)
                scale[p] = jnp.where(sub == i, inv, scale[p])
                ri, fi = over_rows(r[p], i), over_rows(f[p], i)
                if i < 7:
                    m = jnp.where(sub > i, b[p][i] * inv, 0.0)
                    r[p] = r[p] - m * ri
                    f[p] = f[p] - m * fi
                bk = [None] * 8
                for k in range(i + 1, 8):
                    bk[k] = over_rows(b[p][k], i)
                    b[p][k] = b[p][k] - m * bk[k]
                if more:
                    mq = q[p][i] * inv
                    r1[p] = r1[p] - mq * ri
                    f1[p] = f1[p] - mq * fi
                    for k in range(i + 1, 8):
                        q[p][k] = q[p][k] - mq * bk[k]
                    for k in range(8):
                        bn[p][k] = bn[p][k] - mq * over_rows(q[p][i], k)
        for p in range(n):
            root = jnp.sqrt(scale[p])
            y, z = r[p] * root, f[p] * root
            out[p].append(z)
            if more:
                a[p][s + 1], e[p][s + 1] = r1[p], f1[p]
                b[p] = bn[p]
            if s < 14:
                u = dot_tn(y, jnp.concatenate([y, z], axis=1), HIGH)
                for t in range(s + 2, 16):
                    a[p][t] = a[p][t] - u[8 * t : 8 * t + 8, :128]
                    e[p][t] = e[p][t] - u[8 * t : 8 * t + 8, 128:]
    return [jnp.concatenate(o, axis=0) for o in out]


def dispatch_kernel(cap, fix_ref, prev_ref, target_ref, id_ref, rows_ref, send_ref, slot_ref):
    count = rows_ref.shape[0]
    owners = send_ref.shape[0] // cap
    prior = dot_nt(prev_ref[...], fix_ref[...])
    resid = (target_ref[...] - prior).astype(BF16)
    ids = id_ref[...]
    owner = ids // MEM_DEV
    local = ids - owner * MEM_DEV
    hot = lax.broadcasted_iota(jnp.int32, (owners, count), 0) == owner
    before = (
        lax.broadcasted_iota(jnp.int32, (count, count), 0)
        < lax.broadcasted_iota(jnp.int32, (count, count), 1)
    ).astype(BF16)
    ahead = dot_nn(hot.astype(BF16), before)
    place = jnp.sum(jnp.where(hot, ahead, 0.0), axis=0, keepdims=True)
    slot = owner * cap + place.astype(jnp.int32)
    slot_ref[...] = slot
    kind = lax.broadcasted_iota(jnp.int32, (128, count), 0)
    meta = jnp.where(
        kind == 0,
        jnp.broadcast_to(resid.astype(F32), (128, count)),
        (kind == local + 1).astype(F32),
    ).astype(BF16)
    rows = rows_ref[...]
    for c in range(owners * cap // 256):
        pick = (
            lax.broadcasted_iota(jnp.int32, (256, count), 0) + 256 * c == slot
        ).astype(BF16)
        send_ref[256 * c : 256 * c + 256, :MEM] = dot_nn(pick, rows).astype(BF16)
        send_ref[256 * c : 256 * c + 256, MEM:] = dot_nt(pick, meta).astype(BF16)


def member_kernel(recv_ref, coef_ref, score_ref, turned_ref, gram_ref, rhs_ref):
    slots = recv_ref.shape[0]
    unit = (
        lax.broadcasted_iota(jnp.int32, (PAY, PAY), 0)
        == lax.broadcasted_iota(jnp.int32, (PAY, PAY), 1)
    ).astype(BF16)
    for c in range(slots // 256):
        turned_ref[:, 256 * c : 256 * c + 256] = dot_nt(
            unit, recv_ref[256 * c : 256 * c + 256, :]
        ).astype(BF16)
    rows = recv_ref[:, :MEM]
    hots = turned_ref[MEM + 1 : MEM + 1 + MEM_DEV, :]
    resid = turned_ref[MEM : MEM + 1, :]
    rhs_ref[...] = dot_nn(hots * resid, rows)
    ridge = jnp.where(
        lax.broadcasted_iota(jnp.int32, (MEM, MEM), 0)
        == lax.broadcasted_iota(jnp.int32, (MEM, MEM), 1),
        RIDGE_MEMBER,
        0.0,
    )
    for m in range(MEM_DEV):
        gram_ref[m] = dot_nn(turned_ref[:MEM, :] * hots[m : m + 1, :], rows) + ridge

    def solve(p, carry):
        base = GROUP * p
        grams = [gram_ref[base + i] for i in range(GROUP)]
        w0 = factor128([g[:128, :128] for g in grams])
        l10 = [dot_nt(g[128:, :128], w, HIGH) for g, w in zip(grams, w0)]
        w1 = factor128([g[128:, 128:] - dot_nt(l, l, HIGH) for g, l in zip(grams, l10)])
        for i in range(GROUP):
            right = rhs_ref[pl.ds(base + i, 1), :]
            y0 = dot_nt(right[:, :128], w0[i], HIGH)
            y1 = dot_nt(right[:, 128:] - dot_nt(y0, l10[i], HIGH), w1[i], HIGH)
            x1 = dot_nn(y1, w1[i], HIGH)
            x0 = dot_nn(y0 - dot_nn(x1, l10[i], HIGH), w0[i], HIGH)
            coef_ref[pl.ds(base + i, 1), :] = jnp.concatenate([x0, x1], axis=1)
        return carry

    lax.fori_loop(0, MEM_DEV // GROUP, solve, 0)
    low = coef_ref[...].astype(BF16)
    projected = dot_nn(low, turned_ref[:MEM, :])
    score_ref[...] = jnp.sum(projected * hots.astype(F32), axis=0, keepdims=True)


def combine_kernel(back_ref, slot_ref, target_ref, score_ref, resid_ref):
    slots, count = back_ref.shape[1], slot_ref.shape[1]
    parts = split3(back_ref[...])
    stack = jnp.concatenate([part.astype(F32) for part in parts] + [jnp.zeros((5, slots), F32)], axis=0).astype(BF16)
    slot = slot_ref[...]
    total = jnp.zeros((8, count), F32)
    for c in range(slots // 256):
        pick = (
            lax.broadcasted_iota(jnp.int32, (256, count), 0) + 256 * c == slot
        ).astype(BF16)
        total = total + dot_nn(stack[:, 256 * c : 256 * c + 256], pick)
    score = total[0:1] + (total[1:2] + total[2:3])
    score_ref[...] = score
    resid_ref[...] = (target_ref[...] - score).astype(BF16)


def gram_kernel(hi_ref, lo_ref, own_i, own_j, other_i, other_j, out_ref):
    block = dot_tn(own_i[...], own_j[...]) + dot_tn(other_i[...], other_j[...])
    out_ref[:32, 0] = block[:, :128].reshape(32, 8, 128)
    out_ref[32:, 0] = block[:, 128:].reshape(32, 8, 128)


def gram_blocks(own, other, hi, lo):
    rows = own.shape[0]
    tall = lambda pick: pl.BlockSpec((rows, BLK), pick)
    return pl.pallas_call(
        gram_kernel,
        out_shape=jax.ShapeDtypeStruct((64, CORE_PAIRS, 8, 128), F32),
        grid_spec=pltpu.PrefetchScalarGridSpec(
            num_scalar_prefetch=2,
            grid=(CORE_PAIRS,),
            in_specs=[
                tall(lambda b, hi, lo: (0, hi[b])),
                tall(lambda b, hi, lo: (0, lo[b])),
                tall(lambda b, hi, lo: (0, hi[b])),
                tall(lambda b, hi, lo: (0, lo[b])),
            ],
            out_specs=pl.BlockSpec((64, 1, 8, 128), lambda b, hi, lo: (0, b, 0, 0)),
        ),
        compiler_params=params(32),
        name="gram",
    )(hi, lo, own, own, other, other)


def place_of(i, j):
    return i * (i + 1) // 2 + j


def read_block(a_ref, at):
    flat = a_ref[at].reshape(2 * BLK, 128)
    return jnp.concatenate([flat[:BLK], flat[BLK:]], axis=1)


def write_block(a_ref, at, value):
    a_ref[at] = jnp.concatenate([value[:, :128], value[:, 128:]], axis=0).reshape(64, 8, 128)


def factor_kernel(gram_ref, a_ref, w_ref, left_ref, right_ref, sems):
    copies = []
    for core, pairs in enumerate(pair_table()):
        for b, (i, j) in enumerate(pairs):
            at = place_of(i, j)
            copies.append(
                pltpu.make_async_copy(gram_ref.at[:, core, b], a_ref.at[at], sems.at[at])
            )
    for copy in copies:
        copy.start()
    for copy in copies:
        copy.wait()
    ridge = jnp.where(
        lax.broadcasted_iota(jnp.int32, (128, 128), 0)
        == lax.broadcasted_iota(jnp.int32, (128, 128), 1),
        RIDGE_FIXED,
        0.0,
    )

    def step(k, carry):
        diag = a_ref[place_of(k, k)].reshape(2 * BLK, 128)
        w00 = factor128([diag[:128] + ridge])[0]
        l10 = dot_nt(diag[128:256], w00, HIGH)
        w11 = factor128([diag[384:] + ridge - dot_nt(l10, l10, HIGH)])[0]
        w10 = -dot_nn(w11, dot_nn(l10, w00, HIGH), HIGH)
        w_ref[k, :128, :128] = w00
        w_ref[k, :128, 128:] = jnp.zeros((128, 128), F32)
        w_ref[k, 128:, :128] = w10
        w_ref[k, 128:, 128:] = w11
        whole = w_ref[k]

        def panel(i, carry):
            at = place_of(i, k)
            value = dot_nt(read_block(a_ref, at), whole, HIGH)
            write_block(a_ref, at, value)
            h, m, l = split3(value)
            left_ref[i] = jnp.concatenate([h, h, m, h, l, m], axis=1)
            right_ref[i] = jnp.concatenate([h, m, h, l, h, m], axis=1)
            return carry

        lax.fori_loop(k + 1, NBLK, panel, 0)

        def trail_row(i, carry):
            def trail(j, carry):
                at = place_of(i, j)
                gain = dot_nt(left_ref[i], right_ref[j])
                flat = jnp.concatenate([gain[:, :128], gain[:, 128:]], axis=0)
                a_ref[at] = a_ref[at] - flat.reshape(64, 8, 128)
                return carry

            return lax.fori_loop(k + 1, i + 1, trail, carry)

        return lax.fori_loop(k + 1, NBLK, trail_row, carry)

    lax.fori_loop(0, NBLK, step, 0)


def factor_fixed(gram):
    count = NBLK * (NBLK + 1) // 2
    return pl.pallas_call(
        factor_kernel,
        out_shape=(
            jax.ShapeDtypeStruct((count, 64, 8, 128), F32),
            jax.ShapeDtypeStruct((NBLK, BLK, BLK), F32),
        ),
        in_specs=[pl.BlockSpec(memory_space=pl.ANY)],
        out_specs=(
            pl.BlockSpec(memory_space=pltpu.VMEM),
            pl.BlockSpec(memory_space=pltpu.VMEM),
        ),
        scratch_shapes=[
            pltpu.VMEM((NBLK, BLK, 6 * BLK), BF16),
            pltpu.VMEM((NBLK, BLK, 6 * BLK), BF16),
            pltpu.SemaphoreType.DMA((count,)),
        ],
        compiler_params=params(),
        name="factor_fixed",
    )(gram)


def solve_kernel(a_ref, w_ref, grad_ref, fix_ref, member_ref, coef_ref, score_ref):
    forward = []
    for k in range(NBLK):
        part = grad_ref[:, BLK * k : BLK * k + BLK]
        for j in range(k):
            part = part - dot_nt(forward[j], read_block(a_ref, place_of(k, j)), HIGH)
        forward.append(dot_nt(part, w_ref[k], HIGH))
    backward = [None] * NBLK
    for k in range(NBLK - 1, -1, -1):
        part = forward[k]
        for i in range(k + 1, NBLK):
            part = part - dot_nn(backward[i], read_block(a_ref, place_of(i, k)), HIGH)
        backward[k] = dot_nn(part, w_ref[k], HIGH)
    coef = jnp.concatenate(backward, axis=1)
    coef_ref[...] = coef
    score_ref[...] = dot_nt(coef.astype(BF16), fix_ref[...]) + member_ref[...]


def device_sum(value):
    for axes, size in ((("y", "core"), 8), (("z", "x"), 16)):
        spread = jnp.broadcast_to(value[None], (size,) + value.shape)
        value = jnp.sum(lax.all_to_all(spread, axes, split_axis=0, concat_axis=0, tiled=True), axis=0)
    return value


def shards(fixed_rows, member_rows, target, fixed_prev, member_id):
    count = fixed_rows.shape[0]
    devices = lax.axis_size(ALL)
    cap = 3 * count // devices
    slots = devices * cap
    core = lax.axis_index("core")
    swap = [(0, 1), (1, 0)]
    other = lax.ppermute(fixed_rows, "core", swap)

    target_row = target.reshape(1, count)
    send, slot = pl.pallas_call(
        functools.partial(dispatch_kernel, cap),
        out_shape=(
            jax.ShapeDtypeStruct((slots, PAY), BF16),
            jax.ShapeDtypeStruct((1, count), jnp.int32),
        ),
        compiler_params=params(),
        name="dispatch",
    )(fixed_rows, fixed_prev.reshape(1, FIX), target_row, member_id.reshape(1, count), member_rows)
    recv = lax.all_to_all(send.reshape(devices, cap, PAY), ALL, split_axis=0, concat_axis=0, tiled=True)

    table = jnp.array(pair_table(), jnp.int32)[core]
    gram = gram_blocks(fixed_rows, other, table[:, 0], table[:, 1])
    shares = lax.all_to_all(gram, CHIPS, split_axis=0, concat_axis=0, tiled=True)
    share = jnp.sum(shares, axis=0)
    whole = lax.all_gather(share, ALL, axis=0, tiled=False)
    whole = whole.reshape(devices // 2, 2, CORE_PAIRS, 8, 128)

    member_coef, slot_score = pl.pallas_call(
        member_kernel,
        out_shape=(
            jax.ShapeDtypeStruct((MEM_DEV, MEM), F32),
            jax.ShapeDtypeStruct((1, slots), F32),
        ),
        scratch_shapes=[
            pltpu.VMEM((PAY, slots), BF16),
            pltpu.VMEM((MEM_DEV, MEM, MEM), F32),
            pltpu.VMEM((MEM_DEV, MEM), F32),
        ],
        compiler_params=params(),
        name="members",
    )(recv.reshape(slots, PAY))
    back = lax.all_to_all(slot_score.reshape(devices, cap), ALL, split_axis=0, concat_axis=0, tiled=True)
    member_score, fixed_resid = pl.pallas_call(
        combine_kernel,
        out_shape=(
            jax.ShapeDtypeStruct((1, count), F32),
            jax.ShapeDtypeStruct((1, count), BF16),
        ),
        compiler_params=params(),
        name="combine",
    )(back.reshape(1, slots), slot, target_row)
    gradient = device_sum(dot_nn(fixed_resid, fixed_rows))

    lower, inverses = factor_fixed(whole)
    fixed_coef, row_scores = pl.pallas_call(
        solve_kernel,
        out_shape=(
            jax.ShapeDtypeStruct((1, FIX), F32),
            jax.ShapeDtypeStruct((1, count), F32),
        ),
        compiler_params=params(),
        name="substitute",
    )(lower, inverses, gradient, fixed_rows, member_score)
    return (fixed_coef.reshape(FIX), member_coef, row_scores.reshape(count))


def solution(mesh):
    grid = Mesh(mesh.devices.reshape(4, 4, 4, 2), ALL)
    placed = (P(ALL, None), P(ALL, None), P(ALL), P(), P(ALL))
    return jax.shard_map(
        shards,
        mesh=grid,
        in_specs=placed,
        out_specs=(P(), P(ALL, None), P(ALL)),
        check_vma=False,
    )
```

```python
import functools

import jax
import jax.numpy as jnp
from jax import lax
from jax.experimental import pallas as pl
from jax.experimental.pallas import tpu as pltpu
from jax.sharding import Mesh
from jax.sharding import PartitionSpec as P

F32 = jnp.float32
BF16 = jnp.bfloat16
HIGH = lax.Precision.HIGHEST
ALL = ("z", "x", "y", "core")
CHIPS = ("z", "x", "y")

MEM_DEV = 4
RIDGE_FIXED = 4.0
RIDGE_MEMBER = 1.0

FIX = 2048
MEM = 256
PAY = 384
BLK = 256
NBLK = FIX // BLK
CORE_PAIRS = 18


def pair_table():
    table = []
    for core in range(2):
        pairs = []
        for i in range(4 * core, 4 * core + 4):
            pairs += [(i, (i + k) % NBLK) for k in range(4)]
        pairs += [(0, 4), (1, 5)] if core == 0 else [(6, 2), (7, 3)]
        table.append(sorted((max(p), min(p)) for p in pairs))
    return table


def params(mb=56):
    return pltpu.CompilerParams(vmem_limit_bytes=mb << 20)


def dot_nn(a, b, precision=None):
    return lax.dot_general(a, b, (((1,), (0,)), ((), ())), precision=precision, preferred_element_type=F32)


def dot_nt(a, b, precision=None):
    return lax.dot_general(a, b, (((1,), (1,)), ((), ())), precision=precision, preferred_element_type=F32)


def dot_tn(a, b, precision=None):
    return lax.dot_general(a, b, (((0,), (0,)), ((), ())), precision=precision, preferred_element_type=F32)


def cost(us):
    return pl.CostEstimate(flops=int(us * 1e9), transcendentals=0, bytes_accessed=int(us * 2e6))


def split3(v):
    hi = v.astype(BF16)
    rest = v - hi.astype(F32)
    mid = rest.astype(BF16)
    low = (rest - mid.astype(F32)).astype(BF16)
    return hi, mid, low


def as_left(v, axis):
    h, m, l = split3(v)
    return jnp.concatenate([h, h, m, h, l, m], axis=axis)


def as_right(v, axis):
    h, m, l = split3(v)
    return jnp.concatenate([h, m, h, l, h, m], axis=axis)


def full_nn(a, b):
    return dot_nn(as_left(a, 1), as_right(b, 0))


def full_nt(a, b):
    return dot_nt(as_left(a, 1), as_right(b, 1))


def over_lanes(v, c):
    return jnp.broadcast_to(v[:, c : c + 1], v.shape)


def over_rows(v, i):
    return jnp.broadcast_to(v[i : i + 1, :], v.shape)


def factor128(blocks):
    n = len(blocks)
    sub = lax.broadcasted_iota(jnp.int32, (8, 128), 0)
    lane = lax.broadcasted_iota(jnp.int32, (8, 128), 1)
    a = [[blk[8 * t : 8 * t + 8, :] for t in range(16)] for blk in blocks]
    e = [[(lane == sub + 8 * t).astype(F32) for t in range(16)] for _ in blocks]
    out = [[] for _ in blocks]
    b = [[over_lanes(a[p][0], k) for k in range(8)] for p in range(n)]
    for s in range(16):
        more = s < 15
        r = [a[p][s] for p in range(n)]
        f = [e[p][s] for p in range(n)]
        if more:
            r1 = [a[p][s + 1] for p in range(n)]
            f1 = [e[p][s + 1] for p in range(n)]
            q = [[over_lanes(r1[p], 8 * s + k) for k in range(8)] for p in range(n)]
            bn = [[over_lanes(r1[p], 8 * s + 8 + k) for k in range(8)] for p in range(n)]
        scale = [jnp.zeros((8, 128), F32) for _ in range(n)]
        for i in range(8):
            for p in range(n):
                inv = 1.0 / over_rows(b[p][i], i)
                scale[p] = jnp.where(sub == i, inv, scale[p])
                ri, fi = over_rows(r[p], i), over_rows(f[p], i)
                if i < 7:
                    m = jnp.where(sub > i, b[p][i] * inv, 0.0)
                    r[p] = r[p] - m * ri
                    f[p] = f[p] - m * fi
                bk = [None] * 8
                for k in range(i + 1, 8):
                    bk[k] = over_rows(b[p][k], i)
                    b[p][k] = b[p][k] - m * bk[k]
                if more:
                    mq = q[p][i] * inv
                    r1[p] = r1[p] - mq * ri
                    f1[p] = f1[p] - mq * fi
                    for k in range(i + 1, 8):
                        q[p][k] = q[p][k] - mq * bk[k]
                    for k in range(8):
                        bn[p][k] = bn[p][k] - mq * over_rows(q[p][i], k)
        for p in range(n):
            root = jnp.sqrt(scale[p])
            y, z = r[p] * root, f[p] * root
            out[p].append(z)
            if more:
                a[p][s + 1], e[p][s + 1] = r1[p], f1[p]
                b[p] = bn[p]
            if s < 14:
                both = jnp.concatenate([y, z], axis=1)
                u = dot_tn(as_left(y, 0), as_right(both, 0))
                for t in range(s + 2, 16):
                    a[p][t] = a[p][t] - u[8 * t : 8 * t + 8, :128]
                    e[p][t] = e[p][t] - u[8 * t : 8 * t + 8, 128:]
    return [jnp.concatenate(o, axis=0) for o in out]


def dispatch_kernel(cap, fix_ref, prev_ref, target_ref, id_ref, rows_ref, send_ref, slot_ref):
    count = rows_ref.shape[0]
    owners = send_ref.shape[0] // cap
    prior = dot_nt(prev_ref[...], fix_ref[...])
    resid = (target_ref[...] - prior).astype(BF16)
    ids = id_ref[...]
    owner = ids // MEM_DEV
    local = ids - owner * MEM_DEV
    hot = lax.broadcasted_iota(jnp.int32, (owners, count), 0) == owner
    before = (
        lax.broadcasted_iota(jnp.int32, (count, count), 0)
        < lax.broadcasted_iota(jnp.int32, (count, count), 1)
    ).astype(BF16)
    ahead = dot_nn(hot.astype(BF16), before)
    place = jnp.sum(jnp.where(hot, ahead, 0.0), axis=0, keepdims=True)
    slot = owner * cap + place.astype(jnp.int32)
    slot_ref[...] = slot
    kind = lax.broadcasted_iota(jnp.int32, (128, count), 0)
    meta = jnp.where(
        kind == 0,
        jnp.broadcast_to(resid.astype(F32), (128, count)),
        (kind == local + 1).astype(F32),
    ).astype(BF16)
    rows = rows_ref[...]
    for c in range(owners * cap // 256):
        pick = (
            lax.broadcasted_iota(jnp.int32, (256, count), 0) + 256 * c == slot
        ).astype(BF16)
        send_ref[256 * c : 256 * c + 256, :MEM] = dot_nn(pick, rows).astype(BF16)
        send_ref[256 * c : 256 * c + 256, MEM:] = dot_nt(pick, meta).astype(BF16)


def member_kernel(recv_ref, coef_ref, score_ref, turned_ref, gram_ref, rhs_ref):
    slots = recv_ref.shape[0]
    unit = (
        lax.broadcasted_iota(jnp.int32, (PAY, PAY), 0)
        == lax.broadcasted_iota(jnp.int32, (PAY, PAY), 1)
    ).astype(BF16)
    for c in range(slots // 256):
        turned_ref[:, 256 * c : 256 * c + 256] = dot_nt(
            unit, recv_ref[256 * c : 256 * c + 256, :]
        ).astype(BF16)
    rows = recv_ref[:, :MEM]
    hots = turned_ref[MEM + 1 : MEM + 1 + MEM_DEV, :]
    resid = turned_ref[MEM : MEM + 1, :]
    rhs_ref[...] = dot_nn(hots * resid, rows)
    ridge = jnp.where(
        lax.broadcasted_iota(jnp.int32, (MEM, MEM), 0)
        == lax.broadcasted_iota(jnp.int32, (MEM, MEM), 1),
        RIDGE_MEMBER,
        0.0,
    )
    for m in range(MEM_DEV):
        gram_ref[m] = dot_nn(turned_ref[:MEM, :] * hots[m : m + 1, :], rows) + ridge

    grams = [gram_ref[m] for m in range(MEM_DEV)]
    w0 = factor128([g[:128, :128] for g in grams])
    l10 = [full_nt(g[128:, :128], w) for g, w in zip(grams, w0)]
    w1 = factor128([g[128:, 128:] - full_nt(l, l) for g, l in zip(grams, l10)])
    for m in range(MEM_DEV):
        right = rhs_ref[m : m + 1, :]
        y0 = full_nt(right[:, :128], w0[m])
        y1 = full_nt(right[:, 128:] - full_nt(y0, l10[m]), w1[m])
        x1 = full_nn(y1, w1[m])
        x0 = full_nn(y0 - full_nn(x1, l10[m]), w0[m])
        coef_ref[m : m + 1, :] = jnp.concatenate([x0, x1], axis=1)
    low = coef_ref[...].astype(BF16)
    projected = dot_nn(low, turned_ref[:MEM, :])
    score_ref[...] = jnp.sum(projected * hots.astype(F32), axis=0, keepdims=True)


def combine_kernel(back_ref, slot_ref, target_ref, score_ref, resid_ref):
    slots, count = back_ref.shape[1], slot_ref.shape[1]
    parts = split3(back_ref[...])
    stack = jnp.concatenate([part.astype(F32) for part in parts] + [jnp.zeros((5, slots), F32)], axis=0).astype(BF16)
    slot = slot_ref[...]
    total = jnp.zeros((8, count), F32)
    for c in range(slots // 256):
        pick = (
            lax.broadcasted_iota(jnp.int32, (256, count), 0) + 256 * c == slot
        ).astype(BF16)
        total = total + dot_nn(stack[:, 256 * c : 256 * c + 256], pick)
    score = total[0:1] + (total[1:2] + total[2:3])
    score_ref[...] = score
    resid_ref[...] = (target_ref[...] - score).astype(BF16)


def gram_kernel(hi_ref, lo_ref, own_i, own_j, other_i, other_j, out_ref, turned_ref):
    b = pl.program_id(0)

    @pl.when((b == 0) | (hi_ref[b] != hi_ref[jnp.maximum(b - 1, 0)]))
    def _():
        turned_ref[0] = own_i[...].T
        turned_ref[1] = other_i[...].T

    block = dot_nn(turned_ref[0], own_j[...]) + dot_nn(turned_ref[1], other_j[...])
    out_ref[:32, 0] = block[:, :128].reshape(32, 8, 128)
    out_ref[32:, 0] = block[:, 128:].reshape(32, 8, 128)


def gram_blocks(own, other, hi, lo):
    rows = own.shape[0]
    tall = lambda pick: pl.BlockSpec((rows, BLK), pick)
    return pl.pallas_call(
        gram_kernel,
        out_shape=jax.ShapeDtypeStruct((64, CORE_PAIRS, 8, 128), F32),
        grid_spec=pltpu.PrefetchScalarGridSpec(
            num_scalar_prefetch=2,
            grid=(CORE_PAIRS,),
            in_specs=[
                tall(lambda b, hi, lo: (0, hi[b])),
                tall(lambda b, hi, lo: (0, lo[b])),
                tall(lambda b, hi, lo: (0, hi[b])),
                tall(lambda b, hi, lo: (0, lo[b])),
            ],
            out_specs=pl.BlockSpec((64, 1, 8, 128), lambda b, hi, lo: (0, b, 0, 0)),
            scratch_shapes=[pltpu.VMEM((2, BLK, rows), BF16)],
        ),
        compiler_params=params(),
        name="gram",
        cost_estimate=cost(10),
    )(hi, lo, own, own, other, other)


def place_of(i, j):
    return i * (i + 1) // 2 + j


def read_block(a_ref, at):
    flat = a_ref[at].reshape(2 * BLK, 128)
    return jnp.concatenate([flat[:BLK], flat[BLK:]], axis=1)


def write_block(a_ref, at, value):
    a_ref[at] = jnp.concatenate([value[:, :128], value[:, 128:]], axis=0).reshape(64, 8, 128)


def factor_kernel(gram_ref, a_ref, w_ref, done_ref, left_ref, right_ref, sems):
    copies = []
    for core, pairs in enumerate(pair_table()):
        for b, (i, j) in enumerate(pairs):
            at = place_of(i, j)
            copies.append(
                pltpu.make_async_copy(gram_ref.at[:, core, b], a_ref.at[at], sems.at[at])
            )
    for copy in copies:
        copy.start()
    for copy in copies:
        copy.wait()
    ridge = jnp.where(
        lax.broadcasted_iota(jnp.int32, (128, 128), 0)
        == lax.broadcasted_iota(jnp.int32, (128, 128), 1),
        RIDGE_FIXED,
        0.0,
    )

    def step(k, carry):
        diag = a_ref[place_of(k, k)].reshape(2 * BLK, 128)
        w00 = factor128([diag[:128] + ridge])[0]
        l10 = full_nt(diag[128:256], w00)
        w11 = factor128([diag[384:] + ridge - full_nt(l10, l10)])[0]
        w10 = -full_nn(w11, full_nn(l10, w00))
        w_ref[k, :128, :128] = w00
        w_ref[k, :128, 128:] = jnp.zeros((128, 128), F32)
        w_ref[k, 128:, :128] = w10
        w_ref[k, 128:, 128:] = w11
        whole = as_right(w_ref[k], 1)

        def panel(i, carry):
            at = place_of(i, k)
            value = dot_nt(as_left(read_block(a_ref, at), 1), whole)
            write_block(a_ref, at, value)
            h, m, l = split3(value)
            left_ref[i] = jnp.concatenate([h, h, m, h, l, m], axis=1)
            right_ref[i] = jnp.concatenate([h, m, h, l, h, m], axis=1)
            return carry

        lax.fori_loop(k + 1, NBLK, panel, 0)

        def trail_row(i, carry):
            def trail(j, carry):
                at = place_of(i, j)
                gain = dot_nt(left_ref[i], right_ref[j])
                flat = jnp.concatenate([gain[:, :128], gain[:, 128:]], axis=0)
                a_ref[at] = a_ref[at] - flat.reshape(64, 8, 128)
                return carry

            return lax.fori_loop(k + 1, i + 1, trail, carry)

        return lax.fori_loop(k + 1, NBLK, trail_row, carry)

    lax.fori_loop(0, NBLK, step, 0)
    done_ref[...] = jnp.zeros((8, 128), F32)


def factor_fixed(gram):
    count = NBLK * (NBLK + 1) // 2
    return pl.pallas_call(
        factor_kernel,
        out_shape=(
            jax.ShapeDtypeStruct((count, 64, 8, 128), F32),
            jax.ShapeDtypeStruct((NBLK, BLK, BLK), F32),
            jax.ShapeDtypeStruct((8, 128), F32),
        ),
        in_specs=[pl.BlockSpec(memory_space=pl.ANY)],
        out_specs=(
            pl.BlockSpec(memory_space=pltpu.VMEM),
            pl.BlockSpec(memory_space=pltpu.VMEM),
            pl.BlockSpec(memory_space=pltpu.VMEM),
        ),
        scratch_shapes=[
            pltpu.VMEM((NBLK, BLK, 6 * BLK), BF16),
            pltpu.VMEM((NBLK, BLK, 6 * BLK), BF16),
            pltpu.SemaphoreType.DMA((count,)),
        ],
        compiler_params=params(44),
        name="factor_fixed",
        cost_estimate=cost(100),
    )(gram)


def halves(a_ref, at):
    flat = a_ref[at].reshape(2 * BLK, 128)
    return flat[:BLK], flat[BLK:]


def solve_kernel(a_ref, w_ref, grad_ref, fix_ref, member_ref, coef_ref, score_ref):
    turned = [w_ref[k].T for k in range(NBLK)]

    def times_row(left, right, row):
        return left * row[:, :128] + right * row[:, 128:]

    def as_column(spread):
        return jnp.sum(spread, axis=1, keepdims=True)

    forward = []
    for k in range(NBLK):
        part = grad_ref[:, BLK * k : BLK * k + BLK].T
        if k:
            total = jnp.zeros((BLK, 128), F32)
            for j in range(k):
                left, right = halves(a_ref, place_of(k, j))
                total = total + times_row(left, right, forward[j])
            part = part - as_column(total)
        forward.append(jnp.sum(turned[k] * part, axis=0, keepdims=True))
    backward = [None] * NBLK
    for k in range(NBLK - 1, -1, -1):
        part = forward[k]
        if k + 1 < NBLK:
            total = [jnp.zeros((8, 128), F32) for _ in range(2)]
            for i in range(k + 1, NBLK):
                for h, piece in enumerate(halves(a_ref, place_of(i, k))):
                    gain = (piece * backward[i]).reshape(BLK // 8, 8, 128)
                    total[h] = total[h] + jnp.sum(gain, axis=0)
            part = part - jnp.concatenate(
                [jnp.sum(total[h], axis=0, keepdims=True) for h in range(2)], axis=1
            )
        backward[k] = as_column(times_row(turned[k][:, :128], turned[k][:, 128:], part))
    coef = jnp.concatenate([jnp.broadcast_to(x, (BLK, 128)).T[:1] for x in backward], axis=1)
    coef_ref[...] = coef
    score_ref[...] = dot_nt(coef.astype(BF16), fix_ref[...]) + member_ref[...]


def shards(fixed_rows, member_rows, target, fixed_prev, member_id):
    count = fixed_rows.shape[0]
    devices = lax.axis_size(ALL)
    cap = 3 * count // devices
    slots = devices * cap
    core = lax.axis_index("core")
    swap = [(0, 1), (1, 0)]
    other = lax.ppermute(fixed_rows, "core", swap)

    target_row = target.reshape(1, count)
    send, slot = pl.pallas_call(
        functools.partial(dispatch_kernel, cap),
        out_shape=(
            jax.ShapeDtypeStruct((slots, PAY), BF16),
            jax.ShapeDtypeStruct((1, count), jnp.int32),
        ),
        compiler_params=params(),
        name="dispatch",
        cost_estimate=cost(9),
    )(fixed_rows, fixed_prev.reshape(1, FIX), target_row, member_id.reshape(1, count), member_rows)
    other, send = lax.optimization_barrier((other, send))

    table = jnp.array(pair_table(), jnp.int32)[core]
    gram = gram_blocks(fixed_rows, other, table[:, 0], table[:, 1])
    shares = lax.all_to_all(gram, CHIPS, split_axis=0, concat_axis=0, tiled=True)
    shares, send = lax.optimization_barrier((shares, send))
    recv = lax.all_to_all(send.reshape(devices, cap, PAY), ALL, split_axis=0, concat_axis=0, tiled=True)
    share = jnp.sum(shares, axis=0)
    whole = lax.all_gather(share, ALL, axis=0, tiled=False)
    whole = whole.reshape(devices // 2, 2, CORE_PAIRS, 8, 128)

    member_coef, slot_score = pl.pallas_call(
        member_kernel,
        out_shape=(
            jax.ShapeDtypeStruct((MEM_DEV, MEM), F32),
            jax.ShapeDtypeStruct((1, slots), F32),
        ),
        scratch_shapes=[
            pltpu.VMEM((PAY, slots), BF16),
            pltpu.VMEM((MEM_DEV, MEM, MEM), F32),
            pltpu.VMEM((MEM_DEV, MEM), F32),
        ],
        compiler_params=params(),
        name="members",
        cost_estimate=cost(30),
    )(recv.reshape(slots, PAY))
    back = lax.all_to_all(slot_score.reshape(devices, cap), ALL, split_axis=0, concat_axis=0, tiled=True)
    member_score, fixed_resid = pl.pallas_call(
        combine_kernel,
        out_shape=(
            jax.ShapeDtypeStruct((1, count), F32),
            jax.ShapeDtypeStruct((1, count), BF16),
        ),
        compiler_params=params(),
        name="combine",
        cost_estimate=cost(3),
    )(back.reshape(1, slots), slot, target_row)
    gradient = dot_nn(fixed_resid, fixed_rows)
    spread = jnp.broadcast_to(gradient[None], (devices, 1, FIX))
    gradients = lax.all_to_all(spread, ALL, split_axis=0, concat_axis=0, tiled=True)

    lower, inverses, done = factor_fixed(whole)
    gradients, done = lax.optimization_barrier((gradients, done))
    gradient = jnp.sum(gradients, axis=0)
    fixed_coef, row_scores = pl.pallas_call(
        solve_kernel,
        out_shape=(
            jax.ShapeDtypeStruct((1, FIX), F32),
            jax.ShapeDtypeStruct((1, count), F32),
        ),
        compiler_params=params(24),
        name="substitute",
        cost_estimate=cost(12),
    )(lower, inverses, gradient, fixed_rows, member_score)
    return (fixed_coef.reshape(FIX), member_coef, row_scores.reshape(count))


def solution(mesh):
    grid = Mesh(mesh.devices.reshape(4, 4, 4, 2), ALL)
    placed = (P(ALL, None), P(ALL, None), P(ALL), P(), P(ALL))
    return jax.shard_map(
        shards,
        mesh=grid,
        in_specs=placed,
        out_specs=(P(), P(ALL, None), P(ALL)),
        check_vma=False,
    )
```

```python
import functools

import jax
import jax.numpy as jnp
from jax import lax
from jax.experimental import pallas as pl
from jax.experimental.pallas import tpu as pltpu
from jax.sharding import Mesh
from jax.sharding import PartitionSpec as P

F32 = jnp.float32
BF16 = jnp.bfloat16
HIGH = lax.Precision.HIGHEST
ALL = ("z", "x", "y", "core")
CHIPS = ("z", "x", "y")

MEM_DEV = 4
RIDGE_FIXED = 4.0
RIDGE_MEMBER = 1.0

FIX = 2048
MEM = 256
PAY = 384
BLK = 256
NBLK = FIX // BLK
CORE_PAIRS = 18


def pair_table():
    table = []
    for core in range(2):
        pairs = []
        for i in range(4 * core, 4 * core + 4):
            pairs += [(i, (i + k) % NBLK) for k in range(4)]
        pairs += [(0, 4), (1, 5)] if core == 0 else [(6, 2), (7, 3)]
        table.append(sorted((max(p), min(p)) for p in pairs))
    return table


def params(mb=56):
    return pltpu.CompilerParams(vmem_limit_bytes=mb << 20)


def dot_nn(a, b, precision=None):
    return lax.dot_general(a, b, (((1,), (0,)), ((), ())), precision=precision, preferred_element_type=F32)


def dot_nt(a, b, precision=None):
    return lax.dot_general(a, b, (((1,), (1,)), ((), ())), precision=precision, preferred_element_type=F32)


def dot_tn(a, b, precision=None):
    return lax.dot_general(a, b, (((0,), (0,)), ((), ())), precision=precision, preferred_element_type=F32)


def cost(us):
    return pl.CostEstimate(flops=int(us * 1e9), transcendentals=0, bytes_accessed=int(us * 2e6))


def split3(v):
    hi = v.astype(BF16)
    rest = v - hi.astype(F32)
    mid = rest.astype(BF16)
    low = (rest - mid.astype(F32)).astype(BF16)
    return hi, mid, low


def as_left(v, axis):
    h, m, l = split3(v)
    return jnp.concatenate([h, h, m, h, l, m], axis=axis)


def as_right(v, axis):
    h, m, l = split3(v)
    return jnp.concatenate([h, m, h, l, h, m], axis=axis)


def full_nn(a, b):
    return dot_nn(as_left(a, 1), as_right(b, 0))


def full_nt(a, b):
    return dot_nt(as_left(a, 1), as_right(b, 1))


def over_lanes(v, c):
    return jnp.broadcast_to(v[:, c : c + 1], v.shape)


def over_rows(v, i):
    return jnp.broadcast_to(v[i : i + 1, :], v.shape)


def factor128(blocks):
    n = len(blocks)
    sub = lax.broadcasted_iota(jnp.int32, (8, 128), 0)
    lane = lax.broadcasted_iota(jnp.int32, (8, 128), 1)
    a = [[blk[8 * t : 8 * t + 8, :] for t in range(16)] for blk in blocks]
    e = [[(lane == sub + 8 * t).astype(F32) for t in range(16)] for _ in blocks]
    out = [[] for _ in blocks]
    b = [[over_lanes(a[p][0], k) for k in range(8)] for p in range(n)]
    for s in range(16):
        more = s < 15
        r = [a[p][s] for p in range(n)]
        f = [e[p][s] for p in range(n)]
        if more:
            r1 = [a[p][s + 1] for p in range(n)]
            f1 = [e[p][s + 1] for p in range(n)]
            q = [[over_lanes(r1[p], 8 * s + k) for k in range(8)] for p in range(n)]
            bn = [[over_lanes(r1[p], 8 * s + 8 + k) for k in range(8)] for p in range(n)]
        scale = [jnp.zeros((8, 128), F32) for _ in range(n)]
        for i in range(8):
            for p in range(n):
                inv = 1.0 / over_rows(b[p][i], i)
                scale[p] = jnp.where(sub == i, inv, scale[p])
                ri, fi = over_rows(r[p], i), over_rows(f[p], i)
                if i < 7:
                    m = jnp.where(sub > i, b[p][i] * inv, 0.0)
                    r[p] = r[p] - m * ri
                    f[p] = f[p] - m * fi
                bk = [None] * 8
                for k in range(i + 1, 8):
                    bk[k] = over_rows(b[p][k], i)
                    b[p][k] = b[p][k] - m * bk[k]
                if more:
                    mq = q[p][i] * inv
                    r1[p] = r1[p] - mq * ri
                    f1[p] = f1[p] - mq * fi
                    for k in range(i + 1, 8):
                        q[p][k] = q[p][k] - mq * bk[k]
                    for k in range(8):
                        bn[p][k] = bn[p][k] - mq * over_rows(q[p][i], k)
        for p in range(n):
            root = jnp.sqrt(scale[p])
            y, z = r[p] * root, f[p] * root
            out[p].append(z)
            if more:
                a[p][s + 1], e[p][s + 1] = r1[p], f1[p]
                b[p] = bn[p]
            if s < 14:
                both = jnp.concatenate([y, z], axis=1)
                u = dot_tn(as_left(y, 0), as_right(both, 0))
                for t in range(s + 2, 16):
                    a[p][t] = a[p][t] - u[8 * t : 8 * t + 8, :128]
                    e[p][t] = e[p][t] - u[8 * t : 8 * t + 8, 128:]
    return [jnp.concatenate(o, axis=0) for o in out]


def dispatch_kernel(cap, fix_ref, prev_ref, target_ref, id_ref, rows_ref, send_ref, slot_ref):
    count = rows_ref.shape[0]
    owners = send_ref.shape[0] // cap
    prior = dot_nt(prev_ref[...], fix_ref[...])
    resid = (target_ref[...] - prior).astype(BF16)
    ids = id_ref[...]
    owner = ids // MEM_DEV
    local = ids - owner * MEM_DEV
    hot = lax.broadcasted_iota(jnp.int32, (owners, count), 0) == owner
    before = (
        lax.broadcasted_iota(jnp.int32, (count, count), 0)
        < lax.broadcasted_iota(jnp.int32, (count, count), 1)
    ).astype(BF16)
    ahead = dot_nn(hot.astype(BF16), before)
    place = jnp.sum(jnp.where(hot, ahead, 0.0), axis=0, keepdims=True)
    slot = owner * cap + place.astype(jnp.int32)
    slot_ref[...] = slot
    kind = lax.broadcasted_iota(jnp.int32, (128, count), 0)
    meta = jnp.where(
        kind == 0,
        jnp.broadcast_to(resid.astype(F32), (128, count)),
        (kind == local + 1).astype(F32),
    ).astype(BF16)
    rows = rows_ref[...]
    for c in range(owners * cap // 256):
        pick = (
            lax.broadcasted_iota(jnp.int32, (256, count), 0) + 256 * c == slot
        ).astype(BF16)
        send_ref[256 * c : 256 * c + 256, :MEM] = dot_nn(pick, rows).astype(BF16)
        send_ref[256 * c : 256 * c + 256, MEM:] = dot_nt(pick, meta).astype(BF16)


def member_kernel(recv_ref, coef_ref, score_ref, turned_ref, gram_ref, rhs_ref):
    slots = recv_ref.shape[0]
    unit = (
        lax.broadcasted_iota(jnp.int32, (PAY, PAY), 0)
        == lax.broadcasted_iota(jnp.int32, (PAY, PAY), 1)
    ).astype(BF16)
    for c in range(slots // 256):
        turned_ref[:, 256 * c : 256 * c + 256] = dot_nt(
            unit, recv_ref[256 * c : 256 * c + 256, :]
        ).astype(BF16)
    rows = recv_ref[:, :MEM]
    hots = turned_ref[MEM + 1 : MEM + 1 + MEM_DEV, :]
    resid = turned_ref[MEM : MEM + 1, :]
    rhs_ref[...] = dot_nn(hots * resid, rows)
    ridge = jnp.where(
        lax.broadcasted_iota(jnp.int32, (MEM, MEM), 0)
        == lax.broadcasted_iota(jnp.int32, (MEM, MEM), 1),
        RIDGE_MEMBER,
        0.0,
    )
    for m in range(MEM_DEV):
        gram_ref[m] = dot_nn(turned_ref[:MEM, :] * hots[m : m + 1, :], rows) + ridge

    grams = [gram_ref[m] for m in range(MEM_DEV)]
    w0 = factor128([g[:128, :128] for g in grams])
    l10 = [full_nt(g[128:, :128], w) for g, w in zip(grams, w0)]
    w1 = factor128([g[128:, 128:] - full_nt(l, l) for g, l in zip(grams, l10)])
    for m in range(MEM_DEV):
        right = rhs_ref[m : m + 1, :]
        y0 = full_nt(right[:, :128], w0[m])
        y1 = full_nt(right[:, 128:] - full_nt(y0, l10[m]), w1[m])
        x1 = full_nn(y1, w1[m])
        x0 = full_nn(y0 - full_nn(x1, l10[m]), w0[m])
        coef_ref[m : m + 1, :] = jnp.concatenate([x0, x1], axis=1)
    low = coef_ref[...].astype(BF16)
    projected = dot_nn(low, turned_ref[:MEM, :])
    score_ref[...] = jnp.sum(projected * hots.astype(F32), axis=0, keepdims=True)


def combine_kernel(back_ref, slot_ref, target_ref, score_ref, resid_ref):
    slots, count = back_ref.shape[1], slot_ref.shape[1]
    parts = split3(back_ref[...])
    stack = jnp.concatenate([part.astype(F32) for part in parts] + [jnp.zeros((5, slots), F32)], axis=0).astype(BF16)
    slot = slot_ref[...]
    total = jnp.zeros((8, count), F32)
    for c in range(slots // 256):
        pick = (
            lax.broadcasted_iota(jnp.int32, (256, count), 0) + 256 * c == slot
        ).astype(BF16)
        total = total + dot_nn(stack[:, 256 * c : 256 * c + 256], pick)
    score = total[0:1] + (total[1:2] + total[2:3])
    score_ref[...] = score
    resid_ref[...] = (target_ref[...] - score).astype(BF16)


def gram_kernel(hi_ref, lo_ref, own_ref, other_ref, out_ref, turned_ref):
    rows = own_ref.shape[0]
    unit = (
        lax.broadcasted_iota(jnp.int32, (BLK, BLK), 0)
        == lax.broadcasted_iota(jnp.int32, (BLK, BLK), 1)
    ).astype(BF16)
    for part, ref in enumerate((own_ref, other_ref)):
        for i in range(NBLK):
            turned_ref[i, :, rows * part : rows * part + rows] = dot_nt(
                unit, ref[:, BLK * i : BLK * i + BLK]
            ).astype(BF16)

    def block(b, carry):
        left = turned_ref[hi_ref[b]]
        lanes = pl.ds(pl.multiple_of(lo_ref[b] * BLK, BLK), BLK)
        value = dot_nn(left[:, :rows], own_ref[:, lanes]) + dot_nn(left[:, rows:], other_ref[:, lanes])
        out_ref[:32, b] = value[:, :128].reshape(32, 8, 128)
        out_ref[32:, b] = value[:, 128:].reshape(32, 8, 128)
        return carry

    lax.fori_loop(0, CORE_PAIRS, block, 0)


def gram_blocks(own, other, hi, lo):
    rows = own.shape[0]
    return pl.pallas_call(
        gram_kernel,
        out_shape=jax.ShapeDtypeStruct((64, CORE_PAIRS, 8, 128), F32),
        in_specs=[pl.BlockSpec(memory_space=pltpu.SMEM)] * 2
        + [pl.BlockSpec(memory_space=pltpu.VMEM)] * 2,
        out_specs=pl.BlockSpec(memory_space=pltpu.VMEM),
        scratch_shapes=[pltpu.VMEM((NBLK, BLK, 2 * rows), BF16)],
        compiler_params=params(28),
        name="gram",
        cost_estimate=cost(10),
    )(hi, lo, own, other)


def place_of(i, j):
    return i * (i + 1) // 2 + j


def read_block(a_ref, at):
    flat = a_ref[at].reshape(2 * BLK, 128)
    return jnp.concatenate([flat[:BLK], flat[BLK:]], axis=1)


def write_block(a_ref, at, value):
    a_ref[at] = jnp.concatenate([value[:, :128], value[:, 128:]], axis=0).reshape(64, 8, 128)


def factor_kernel(gram_ref, a_ref, w_ref, done_ref, left_ref, right_ref, sems):
    copies = []
    for core, pairs in enumerate(pair_table()):
        for b, (i, j) in enumerate(pairs):
            at = place_of(i, j)
            copies.append(
                pltpu.make_async_copy(gram_ref.at[:, core, b], a_ref.at[at], sems.at[at])
            )
    for copy in copies:
        copy.start()
    for copy in copies:
        copy.wait()
    ridge = jnp.where(
        lax.broadcasted_iota(jnp.int32, (128, 128), 0)
        == lax.broadcasted_iota(jnp.int32, (128, 128), 1),
        RIDGE_FIXED,
        0.0,
    )

    def step(k, carry):
        diag = a_ref[place_of(k, k)].reshape(2 * BLK, 128)
        w00 = factor128([diag[:128] + ridge])[0]
        l10 = full_nt(diag[128:256], w00)
        w11 = factor128([diag[384:] + ridge - full_nt(l10, l10)])[0]
        w10 = -full_nn(w11, full_nn(l10, w00))
        w_ref[k, :128, :128] = w00
        w_ref[k, :128, 128:] = jnp.zeros((128, 128), F32)
        w_ref[k, 128:, :128] = w10
        w_ref[k, 128:, 128:] = w11
        whole = as_right(w_ref[k], 1)

        def panel(i, carry):
            at = place_of(i, k)
            value = dot_nt(as_left(read_block(a_ref, at), 1), whole)
            write_block(a_ref, at, value)
            h, m, l = split3(value)
            left_ref[i] = jnp.concatenate([h, h, m, h, l, m], axis=1)
            right_ref[i] = jnp.concatenate([h, m, h, l, h, m], axis=1)
            return carry

        lax.fori_loop(k + 1, NBLK, panel, 0)

        def trail_row(i, carry):
            def trail(j, carry):
                at = place_of(i, j)
                gain = dot_nt(left_ref[i], right_ref[j])
                flat = jnp.concatenate([gain[:, :128], gain[:, 128:]], axis=0)
                a_ref[at] = a_ref[at] - flat.reshape(64, 8, 128)
                return carry

            return lax.fori_loop(k + 1, i + 1, trail, carry)

        return lax.fori_loop(k + 1, NBLK, trail_row, carry)

    lax.fori_loop(0, NBLK, step, 0)
    done_ref[...] = jnp.zeros((8, 128), F32)


def factor_fixed(gram):
    count = NBLK * (NBLK + 1) // 2
    return pl.pallas_call(
        factor_kernel,
        out_shape=(
            jax.ShapeDtypeStruct((count, 64, 8, 128), F32),
            jax.ShapeDtypeStruct((NBLK, BLK, BLK), F32),
            jax.ShapeDtypeStruct((8, 128), F32),
        ),
        in_specs=[pl.BlockSpec(memory_space=pl.ANY)],
        out_specs=(
            pl.BlockSpec(memory_space=pltpu.VMEM),
            pl.BlockSpec(memory_space=pltpu.VMEM),
            pl.BlockSpec(memory_space=pltpu.VMEM),
        ),
        scratch_shapes=[
            pltpu.VMEM((NBLK, BLK, 6 * BLK), BF16),
            pltpu.VMEM((NBLK, BLK, 6 * BLK), BF16),
            pltpu.SemaphoreType.DMA((count,)),
        ],
        compiler_params=params(44),
        name="factor_fixed",
        cost_estimate=cost(100),
    )(gram)


def halves(a_ref, at):
    flat = a_ref[at].reshape(2 * BLK, 128)
    return flat[:BLK], flat[BLK:]


def solve_kernel(a_ref, w_ref, grad_ref, fix_ref, member_ref, coef_ref, score_ref):
    turned = [w_ref[k].T for k in range(NBLK)]

    def times_row(left, right, row):
        return left * row[:, :128] + right * row[:, 128:]

    def as_column(spread):
        return jnp.sum(spread, axis=1, keepdims=True)

    forward = []
    for k in range(NBLK):
        part = grad_ref[:, BLK * k : BLK * k + BLK].T
        if k:
            total = jnp.zeros((BLK, 128), F32)
            for j in range(k):
                left, right = halves(a_ref, place_of(k, j))
                total = total + times_row(left, right, forward[j])
            part = part - as_column(total)
        forward.append(jnp.sum(turned[k] * part, axis=0, keepdims=True))
    backward = [None] * NBLK
    for k in range(NBLK - 1, -1, -1):
        part = forward[k]
        if k + 1 < NBLK:
            total = [jnp.zeros((8, 128), F32) for _ in range(2)]
            for i in range(k + 1, NBLK):
                for h, piece in enumerate(halves(a_ref, place_of(i, k))):
                    gain = (piece * backward[i]).reshape(BLK // 8, 8, 128)
                    total[h] = total[h] + jnp.sum(gain, axis=0)
            part = part - jnp.concatenate(
                [jnp.sum(total[h], axis=0, keepdims=True) for h in range(2)], axis=1
            )
        backward[k] = as_column(times_row(turned[k][:, :128], turned[k][:, 128:], part))
    coef = jnp.concatenate([jnp.broadcast_to(x, (BLK, 128)).T[:1] for x in backward], axis=1)
    coef_ref[...] = coef
    score_ref[...] = dot_nt(coef.astype(BF16), fix_ref[...]) + member_ref[...]


def shards(fixed_rows, member_rows, target, fixed_prev, member_id):
    count = fixed_rows.shape[0]
    devices = lax.axis_size(ALL)
    cap = 3 * count // devices
    slots = devices * cap
    core = lax.axis_index("core")
    swap = [(0, 1), (1, 0)]
    other = lax.ppermute(fixed_rows, "core", swap)

    target_row = target.reshape(1, count)
    send, slot = pl.pallas_call(
        functools.partial(dispatch_kernel, cap),
        out_shape=(
            jax.ShapeDtypeStruct((slots, PAY), BF16),
            jax.ShapeDtypeStruct((1, count), jnp.int32),
        ),
        compiler_params=params(),
        name="dispatch",
        cost_estimate=cost(9),
    )(fixed_rows, fixed_prev.reshape(1, FIX), target_row, member_id.reshape(1, count), member_rows)
    other, send = lax.optimization_barrier((other, send))

    table = jnp.array(pair_table(), jnp.int32)[core]
    gram = gram_blocks(fixed_rows, other, table[:, 0], table[:, 1])
    shares = lax.all_to_all(gram, CHIPS, split_axis=0, concat_axis=0, tiled=True)
    shares, send = lax.optimization_barrier((shares, send))
    recv = lax.all_to_all(send.reshape(devices, cap, PAY), ALL, split_axis=0, concat_axis=0, tiled=True)
    share = jnp.sum(shares, axis=0)
    whole = lax.all_gather(share, ALL, axis=0, tiled=False)
    whole = whole.reshape(devices // 2, 2, CORE_PAIRS, 8, 128)

    member_coef, slot_score = pl.pallas_call(
        member_kernel,
        out_shape=(
            jax.ShapeDtypeStruct((MEM_DEV, MEM), F32),
            jax.ShapeDtypeStruct((1, slots), F32),
        ),
        scratch_shapes=[
            pltpu.VMEM((PAY, slots), BF16),
            pltpu.VMEM((MEM_DEV, MEM, MEM), F32),
            pltpu.VMEM((MEM_DEV, MEM), F32),
        ],
        compiler_params=params(),
        name="members",
        cost_estimate=cost(30),
    )(recv.reshape(slots, PAY))
    back = lax.all_to_all(slot_score.reshape(devices, cap), ALL, split_axis=0, concat_axis=0, tiled=True)
    member_score, fixed_resid = pl.pallas_call(
        combine_kernel,
        out_shape=(
            jax.ShapeDtypeStruct((1, count), F32),
            jax.ShapeDtypeStruct((1, count), BF16),
        ),
        compiler_params=params(),
        name="combine",
        cost_estimate=cost(3),
    )(back.reshape(1, slots), slot, target_row)
    gradient = dot_nn(fixed_resid, fixed_rows)
    spread = jnp.broadcast_to(gradient[None], (devices, 1, FIX))
    gradients = lax.all_to_all(spread, ALL, split_axis=0, concat_axis=0, tiled=True)

    lower, inverses, done = factor_fixed(whole)
    gradients, done = lax.optimization_barrier((gradients, done))
    gradient = jnp.sum(gradients, axis=0) + done[:1, :1]
    fixed_coef, row_scores = pl.pallas_call(
        solve_kernel,
        out_shape=(
            jax.ShapeDtypeStruct((1, FIX), F32),
            jax.ShapeDtypeStruct((1, count), F32),
        ),
        compiler_params=params(24),
        name="substitute",
        cost_estimate=cost(12),
    )(lower, inverses, gradient, fixed_rows, member_score)
    return (fixed_coef.reshape(FIX), member_coef, row_scores.reshape(count))


def solution(mesh):
    grid = Mesh(mesh.devices.reshape(4, 4, 4, 2), ALL)
    placed = (P(ALL, None), P(ALL, None), P(ALL), P(), P(ALL))
    return jax.shard_map(
        shards,
        mesh=grid,
        in_specs=placed,
        out_specs=(P(), P(ALL, None), P(ALL)),
        check_vma=False,
    )
```

```python
import functools

import jax
import jax.numpy as jnp
from jax import lax
from jax.experimental import pallas as pl
from jax.experimental.pallas import tpu as pltpu
from jax.sharding import Mesh
from jax.sharding import PartitionSpec as P

F32 = jnp.float32
BF16 = jnp.bfloat16
HIGH = lax.Precision.HIGHEST
ALL = ("z", "x", "y", "core")
CHIPS = ("z", "x", "y")

MEM_DEV = 4
RIDGE_FIXED = 4.0
RIDGE_MEMBER = 1.0

FIX = 2048
MEM = 256
PAY = 384
BLK = 256
NBLK = FIX // BLK
CORE_PAIRS = 18


def pair_table():
    table = []
    for core in range(2):
        pairs = []
        for i in range(4 * core, 4 * core + 4):
            pairs += [(i, (i + k) % NBLK) for k in range(4)]
        pairs += [(0, 4), (1, 5)] if core == 0 else [(6, 2), (7, 3)]
        table.append(sorted((max(p), min(p)) for p in pairs))
    return table


def params(mb=56):
    return pltpu.CompilerParams(vmem_limit_bytes=mb << 20)


def dot_nn(a, b, precision=None):
    return lax.dot_general(a, b, (((1,), (0,)), ((), ())), precision=precision, preferred_element_type=F32)


def dot_nt(a, b, precision=None):
    return lax.dot_general(a, b, (((1,), (1,)), ((), ())), precision=precision, preferred_element_type=F32)


def dot_tn(a, b, precision=None):
    return lax.dot_general(a, b, (((0,), (0,)), ((), ())), precision=precision, preferred_element_type=F32)


def cost(us):
    return pl.CostEstimate(flops=int(us * 1e9), transcendentals=0, bytes_accessed=int(us * 2e6))


def split3(v):
    hi = v.astype(BF16)
    rest = v - hi.astype(F32)
    mid = rest.astype(BF16)
    low = (rest - mid.astype(F32)).astype(BF16)
    return hi, mid, low


def as_left(v, axis):
    h, m, l = split3(v)
    return jnp.concatenate([h, h, m, h, l, m], axis=axis)


def as_right(v, axis):
    h, m, l = split3(v)
    return jnp.concatenate([h, m, h, l, h, m], axis=axis)


def full_nn(a, b):
    return dot_nn(as_left(a, 1), as_right(b, 0))


def full_nt(a, b):
    return dot_nt(as_left(a, 1), as_right(b, 1))


def over_lanes(v, c):
    return jnp.broadcast_to(v[:, c : c + 1], v.shape)


def over_rows(v, i):
    return jnp.broadcast_to(v[i : i + 1, :], v.shape)


def factor128(blocks, aside=None):
    n = len(blocks)
    sub = lax.broadcasted_iota(jnp.int32, (8, 128), 0)
    lane = lax.broadcasted_iota(jnp.int32, (8, 128), 1)
    a = [[blk[8 * t : 8 * t + 8, :] for t in range(16)] for blk in blocks]
    e = [[(lane == sub + 8 * t).astype(F32) for t in range(16)] for _ in blocks]
    out = [[] for _ in blocks]
    b = [[over_lanes(a[p][0], k) for k in range(8)] for p in range(n)]
    for s in range(16):
        more = s < 15
        if aside is not None:
            aside(s)
        r = [a[p][s] for p in range(n)]
        f = [e[p][s] for p in range(n)]
        if more:
            r1 = [a[p][s + 1] for p in range(n)]
            f1 = [e[p][s + 1] for p in range(n)]
            q = [[over_lanes(r1[p], 8 * s + k) for k in range(8)] for p in range(n)]
            bn = [[over_lanes(r1[p], 8 * s + 8 + k) for k in range(8)] for p in range(n)]
        scale = [jnp.zeros((8, 128), F32) for _ in range(n)]
        for i in range(8):
            for p in range(n):
                inv = 1.0 / over_rows(b[p][i], i)
                scale[p] = jnp.where(sub == i, inv, scale[p])
                ri, fi = over_rows(r[p], i), over_rows(f[p], i)
                if i < 7:
                    m = jnp.where(sub > i, b[p][i] * inv, 0.0)
                    r[p] = r[p] - m * ri
                    f[p] = f[p] - m * fi
                bk = [None] * 8
                for k in range(i + 1, 8):
                    bk[k] = over_rows(b[p][k], i)
                    b[p][k] = b[p][k] - m * bk[k]
                if more:
                    mq = q[p][i] * inv
                    r1[p] = r1[p] - mq * ri
                    f1[p] = f1[p] - mq * fi
                    for k in range(i + 1, 8):
                        q[p][k] = q[p][k] - mq * bk[k]
                    for k in range(8):
                        bn[p][k] = bn[p][k] - mq * over_rows(q[p][i], k)
        for p in range(n):
            root = jnp.sqrt(scale[p])
            y, z = r[p] * root, f[p] * root
            out[p].append(z)
            if more:
                a[p][s + 1], e[p][s + 1] = r1[p], f1[p]
                b[p] = bn[p]
            if s < 14:
                both = jnp.concatenate([y, z], axis=1)
                u = dot_tn(as_left(y, 0), as_right(both, 0))
                for t in range(s + 2, 16):
                    a[p][t] = a[p][t] - u[8 * t : 8 * t + 8, :128]
                    e[p][t] = e[p][t] - u[8 * t : 8 * t + 8, 128:]
    return [jnp.concatenate(o, axis=0) for o in out]


def dispatch_kernel(cap, fix_ref, prev_ref, target_ref, id_ref, rows_ref, send_ref, slot_ref):
    count = rows_ref.shape[0]
    owners = send_ref.shape[0] // cap
    prior = dot_nt(prev_ref[...], fix_ref[...])
    resid = (target_ref[...] - prior).astype(BF16)
    ids = id_ref[...]
    owner = ids // MEM_DEV
    local = ids - owner * MEM_DEV
    hot = lax.broadcasted_iota(jnp.int32, (owners, count), 0) == owner
    before = (
        lax.broadcasted_iota(jnp.int32, (count, count), 0)
        < lax.broadcasted_iota(jnp.int32, (count, count), 1)
    ).astype(BF16)
    ahead = dot_nn(hot.astype(BF16), before)
    place = jnp.sum(jnp.where(hot, ahead, 0.0), axis=0, keepdims=True)
    slot = owner * cap + place.astype(jnp.int32)
    slot_ref[...] = slot
    kind = lax.broadcasted_iota(jnp.int32, (128, count), 0)
    meta = jnp.where(
        kind == 0,
        jnp.broadcast_to(resid.astype(F32), (128, count)),
        (kind == local + 1).astype(F32),
    ).astype(BF16)
    rows = rows_ref[...]

    def place_rows(c, carry):
        pick = (
            lax.broadcasted_iota(jnp.int32, (256, count), 0) + 256 * c == slot
        ).astype(BF16)
        at = pl.ds(pl.multiple_of(256 * c, 256), 256)
        send_ref[at, :MEM] = dot_nn(pick, rows).astype(BF16)
        send_ref[at, MEM:] = dot_nt(pick, meta).astype(BF16)
        return carry

    lax.fori_loop(0, owners * cap // 256, place_rows, 0)


def member_kernel(recv_ref, coef_ref, score_ref, turned_ref, gram_ref, rhs_ref):
    slots = recv_ref.shape[0]
    unit = (
        lax.broadcasted_iota(jnp.int32, (PAY, PAY), 0)
        == lax.broadcasted_iota(jnp.int32, (PAY, PAY), 1)
    ).astype(BF16)

    def turn(c, carry):
        at = pl.ds(pl.multiple_of(256 * c, 256), 256)
        turned_ref[:, at] = dot_nt(unit, recv_ref[at, :]).astype(BF16)
        return carry

    lax.fori_loop(0, slots // 256, turn, 0)
    rows = recv_ref[:, :MEM]
    hots = turned_ref[MEM + 1 : MEM + 1 + MEM_DEV, :]
    resid = turned_ref[MEM : MEM + 1, :]
    rhs_ref[...] = dot_nn(hots * resid, rows)
    ridge = jnp.where(
        lax.broadcasted_iota(jnp.int32, (MEM, MEM), 0)
        == lax.broadcasted_iota(jnp.int32, (MEM, MEM), 1),
        RIDGE_MEMBER,
        0.0,
    )
    for m in range(MEM_DEV):
        gram_ref[m] = ridge

    def collect(c, carry):
        at = pl.ds(pl.multiple_of(512 * c, 512), 512)
        piece = turned_ref[:MEM, at]
        hot = turned_ref[MEM + 1 : MEM + 1 + MEM_DEV, at]
        tall = jnp.concatenate([piece * hot[m : m + 1] for m in range(MEM_DEV)], axis=0)
        gain = dot_nn(tall, recv_ref[at, :MEM])
        for m in range(MEM_DEV):
            gram_ref[m] = gram_ref[m] + gain[MEM * m : MEM * m + MEM]
        return carry

    lax.fori_loop(0, slots // 512, collect, 0)

    grams = [gram_ref[m] for m in range(MEM_DEV)]
    w0 = factor128([g[:128, :128] for g in grams])
    l10 = [full_nt(g[128:, :128], w) for g, w in zip(grams, w0)]
    w1 = factor128([g[128:, 128:] - full_nt(l, l) for g, l in zip(grams, l10)])
    for m in range(MEM_DEV):
        right = rhs_ref[m : m + 1, :]
        y0 = full_nt(right[:, :128], w0[m])
        y1 = full_nt(right[:, 128:] - full_nt(y0, l10[m]), w1[m])
        x1 = full_nn(y1, w1[m])
        x0 = full_nn(y0 - full_nn(x1, l10[m]), w0[m])
        coef_ref[m : m + 1, :] = jnp.concatenate([x0, x1], axis=1)
    low = coef_ref[...].astype(BF16)
    projected = dot_nn(low, turned_ref[:MEM, :])
    score_ref[...] = jnp.sum(projected * hots.astype(F32), axis=0, keepdims=True)


def combine_kernel(back_ref, slot_ref, target_ref, score_ref, resid_ref):
    slots, count = back_ref.shape[1], slot_ref.shape[1]
    parts = split3(back_ref[...])
    stack = jnp.concatenate([part.astype(F32) for part in parts] + [jnp.zeros((5, slots), F32)], axis=0).astype(BF16)
    slot = slot_ref[...]
    total = jnp.zeros((8, count), F32)
    for c in range(slots // 256):
        pick = (
            lax.broadcasted_iota(jnp.int32, (256, count), 0) + 256 * c == slot
        ).astype(BF16)
        total = total + dot_nn(stack[:, 256 * c : 256 * c + 256], pick)
    score = total[0:1] + (total[1:2] + total[2:3])
    score_ref[...] = score
    resid_ref[...] = (target_ref[...] - score).astype(BF16)


def gram_kernel(hi_ref, lo_ref, own_ref, other_ref, out_ref, turned_ref):
    rows = own_ref.shape[0]
    unit = (
        lax.broadcasted_iota(jnp.int32, (BLK, BLK), 0)
        == lax.broadcasted_iota(jnp.int32, (BLK, BLK), 1)
    ).astype(BF16)

    def turn(i, carry):
        lanes = pl.ds(pl.multiple_of(BLK * i, BLK), BLK)
        turned_ref[i, :, :rows] = dot_nt(unit, own_ref[:, lanes]).astype(BF16)
        turned_ref[i, :, rows:] = dot_nt(unit, other_ref[:, lanes]).astype(BF16)
        return carry

    lax.fori_loop(0, NBLK, turn, 0)

    def block(b, carry):
        left = turned_ref[hi_ref[b]]
        lanes = pl.ds(pl.multiple_of(lo_ref[b] * BLK, BLK), BLK)
        value = dot_nn(left[:, :rows], own_ref[:, lanes]) + dot_nn(left[:, rows:], other_ref[:, lanes])
        out_ref[:32, b] = value[:, :128].reshape(32, 8, 128)
        out_ref[32:, b] = value[:, 128:].reshape(32, 8, 128)
        return carry

    lax.fori_loop(0, CORE_PAIRS, block, 0)


def gram_blocks(own, other, hi, lo):
    rows = own.shape[0]
    return pl.pallas_call(
        gram_kernel,
        out_shape=jax.ShapeDtypeStruct((64, CORE_PAIRS, 8, 128), F32),
        in_specs=[pl.BlockSpec(memory_space=pltpu.SMEM)] * 2
        + [pl.BlockSpec(memory_space=pltpu.VMEM)] * 2,
        out_specs=pl.BlockSpec(memory_space=pltpu.VMEM),
        scratch_shapes=[pltpu.VMEM((NBLK, BLK, 2 * rows), BF16)],
        compiler_params=params(28),
        name="gram",
        cost_estimate=cost(10),
    )(hi, lo, own, other)


def place_of(i, j):
    return i * (i + 1) // 2 + j


def read_block(a_ref, at):
    flat = a_ref[at].reshape(2 * BLK, 128)
    return jnp.concatenate([flat[:BLK], flat[BLK:]], axis=1)


def write_block(a_ref, at, value):
    a_ref[at] = jnp.concatenate([value[:, :128], value[:, 128:]], axis=0).reshape(64, 8, 128)


WIDE = 32
SLIM = 16


def job_table():
    spare = NBLK * (NBLK + 1) // 2
    table = []
    for k in range(NBLK):
        jobs = []
        if k:
            jobs = [(i, j, place_of(i, j)) for i in range(k, NBLK) for j in range(k, i + 1)][1:]
        jobs += [(NBLK - 1, NBLK - 1, spare)] * (WIDE - len(jobs))
        table.append([entry for job in jobs for entry in job])
    return table


def factor_kernel(table_ref, gram_ref, a_ref, w_ref, done_ref, left_ref, right_ref, sems):
    copies = []
    for core, pairs in enumerate(pair_table()):
        for b, (i, j) in enumerate(pairs):
            at = place_of(i, j)
            copies.append(
                pltpu.make_async_copy(gram_ref.at[:, core, b], a_ref.at[at], sems.at[at])
            )
    for copy in copies:
        copy.start()
    for copy in copies:
        copy.wait()
    left_ref[NBLK - 1] = jnp.zeros((BLK, 6 * BLK), BF16)
    right_ref[NBLK - 1] = jnp.zeros((BLK, 6 * BLK), BF16)
    a_ref[NBLK * (NBLK + 1) // 2] = jnp.zeros((64, 8, 128), F32)
    ridge = jnp.where(
        lax.broadcasted_iota(jnp.int32, (128, 128), 0)
        == lax.broadcasted_iota(jnp.int32, (128, 128), 1),
        RIDGE_FIXED,
        0.0,
    )

    def trail(i, j, at):
        gain = dot_nt(left_ref[i], right_ref[j])
        flat = jnp.concatenate([gain[:, :128], gain[:, 128:]], axis=0)
        a_ref[at] = a_ref[at] - flat.reshape(64, 8, 128)

    def diagonal(k, every):
        def aside(first):
            def emit(s):
                if s % every == 0:
                    slot = 3 * (first + s // every)
                    trail(table_ref[k, slot], table_ref[k, slot + 1], table_ref[k, slot + 2])

            return emit

        diag = a_ref[place_of(k, k)].reshape(2 * BLK, 128)
        w00 = factor128([diag[:128] + ridge], aside(0))[0]
        l10 = full_nt(diag[128:256], w00)
        cross = full_nn(l10, w00)
        w11 = factor128([diag[384:] + ridge - full_nt(l10, l10)], aside(16 // every))[0]
        w_ref[k, :128, :128] = w00
        w_ref[k, :128, 128:] = jnp.zeros((128, 128), F32)
        w_ref[k, 128:, :128] = -full_nn(w11, cross)
        w_ref[k, 128:, 128:] = w11

    def step(k, carry):
        wide = (k == 1) | (k == 2)

        @pl.when(wide)
        def _():
            diagonal(k, 1)

        @pl.when(jnp.logical_not(wide))
        def _():
            diagonal(k, 2)

        whole = as_right(w_ref[k], 1)

        def panel(i, carry):
            at = place_of(i, k)
            value = dot_nt(as_left(read_block(a_ref, at), 1), whole)
            write_block(a_ref, at, value)
            h, m, l = split3(value)
            left_ref[i] = jnp.concatenate([h, h, m, h, l, m], axis=1)
            right_ref[i] = jnp.concatenate([h, m, h, l, h, m], axis=1)
            return carry

        lax.fori_loop(k + 1, NBLK, panel, 0)

        @pl.when(k + 1 < NBLK)
        def _():
            trail(k + 1, k + 1, place_of(k + 1, k + 1))

        return carry

    lax.fori_loop(0, NBLK, step, 0)
    done_ref[...] = jnp.zeros((8, 128), F32)


def factor_fixed(gram):
    count = NBLK * (NBLK + 1) // 2
    return pl.pallas_call(
        factor_kernel,
        out_shape=(
            jax.ShapeDtypeStruct((count + 1, 64, 8, 128), F32),
            jax.ShapeDtypeStruct((NBLK, BLK, BLK), F32),
            jax.ShapeDtypeStruct((8, 128), F32),
        ),
        in_specs=[pl.BlockSpec(memory_space=pltpu.SMEM), pl.BlockSpec(memory_space=pl.ANY)],
        out_specs=(
            pl.BlockSpec(memory_space=pltpu.VMEM),
            pl.BlockSpec(memory_space=pltpu.VMEM),
            pl.BlockSpec(memory_space=pltpu.VMEM),
        ),
        scratch_shapes=[
            pltpu.VMEM((NBLK, BLK, 6 * BLK), BF16),
            pltpu.VMEM((NBLK, BLK, 6 * BLK), BF16),
            pltpu.SemaphoreType.DMA((count,)),
        ],
        compiler_params=params(46),
        name="factor_fixed",
        cost_estimate=cost(100),
    )(jnp.array(job_table(), jnp.int32), gram)


def halves(a_ref, at):
    flat = a_ref[at].reshape(2 * BLK, 128)
    return flat[:BLK], flat[BLK:]


def solve_kernel(low_ref, w_ref, grad_ref, fix_ref, member_ref, coef_ref, score_ref, a_ref, sems):
    copies = {}
    for k in range(1, NBLK):
        for j in range(k):
            at = place_of(k, j)
            copies[k, j] = pltpu.make_async_copy(low_ref.at[at], a_ref.at[at], sems.at[at])
            copies[k, j].start()
    turned = [w_ref[k].T for k in range(NBLK)]

    def times_row(left, right, row):
        return left * row[:, :128] + right * row[:, 128:]

    def as_column(spread):
        return jnp.sum(spread, axis=1, keepdims=True)

    forward = []
    for k in range(NBLK):
        part = grad_ref[:, BLK * k : BLK * k + BLK].T
        if k:
            total = jnp.zeros((BLK, 128), F32)
            for j in range(k):
                copies[k, j].wait()
                left, right = halves(a_ref, place_of(k, j))
                total = total + times_row(left, right, forward[j])
            part = part - as_column(total)
        forward.append(jnp.sum(turned[k] * part, axis=0, keepdims=True))
    backward = [None] * NBLK
    for k in range(NBLK - 1, -1, -1):
        part = forward[k]
        if k + 1 < NBLK:
            total = [jnp.zeros((8, 128), F32) for _ in range(2)]
            for i in range(k + 1, NBLK):
                for h, piece in enumerate(halves(a_ref, place_of(i, k))):
                    gain = (piece * backward[i]).reshape(BLK // 8, 8, 128)
                    total[h] = total[h] + jnp.sum(gain, axis=0)
            part = part - jnp.concatenate(
                [jnp.sum(total[h], axis=0, keepdims=True) for h in range(2)], axis=1
            )
        backward[k] = as_column(times_row(turned[k][:, :128], turned[k][:, 128:], part))
    coef = jnp.concatenate([jnp.broadcast_to(x, (BLK, 128)).T[:1] for x in backward], axis=1)
    coef_ref[...] = coef
    score_ref[...] = dot_nt(coef.astype(BF16), fix_ref[...]) + member_ref[...]


def shards(fixed_rows, member_rows, target, fixed_prev, member_id):
    count = fixed_rows.shape[0]
    devices = lax.axis_size(ALL)
    cap = 3 * count // devices
    slots = devices * cap
    core = lax.axis_index("core")
    swap = [(0, 1), (1, 0)]
    other = lax.ppermute(fixed_rows, "core", swap)

    target_row = target.reshape(1, count)
    send, slot = pl.pallas_call(
        functools.partial(dispatch_kernel, cap),
        out_shape=(
            jax.ShapeDtypeStruct((slots, PAY), BF16),
            jax.ShapeDtypeStruct((1, count), jnp.int32),
        ),
        compiler_params=params(),
        name="dispatch",
        cost_estimate=cost(9),
    )(fixed_rows, fixed_prev.reshape(1, FIX), target_row, member_id.reshape(1, count), member_rows)
    other, send = lax.optimization_barrier((other, send))

    table = jnp.array(pair_table(), jnp.int32)[core]
    gram = gram_blocks(fixed_rows, other, table[:, 0], table[:, 1])
    shares = lax.all_to_all(gram, CHIPS, split_axis=0, concat_axis=0, tiled=True)
    shares, send = lax.optimization_barrier((shares, send))
    recv = lax.all_to_all(send.reshape(devices, cap, PAY), ALL, split_axis=0, concat_axis=0, tiled=True)
    share = jnp.sum(shares, axis=0)
    whole = lax.all_gather(share, ALL, axis=0, tiled=False)
    whole = whole.reshape(devices // 2, 2, CORE_PAIRS, 8, 128)

    member_coef, slot_score = pl.pallas_call(
        member_kernel,
        out_shape=(
            jax.ShapeDtypeStruct((MEM_DEV, MEM), F32),
            jax.ShapeDtypeStruct((1, slots), F32),
        ),
        scratch_shapes=[
            pltpu.VMEM((PAY, slots), BF16),
            pltpu.VMEM((MEM_DEV, MEM, MEM), F32),
            pltpu.VMEM((MEM_DEV, MEM), F32),
        ],
        compiler_params=params(),
        name="members",
        cost_estimate=cost(30),
    )(recv.reshape(slots, PAY))
    back = lax.all_to_all(slot_score.reshape(devices, cap), ALL, split_axis=0, concat_axis=0, tiled=True)
    member_score, fixed_resid = pl.pallas_call(
        combine_kernel,
        out_shape=(
            jax.ShapeDtypeStruct((1, count), F32),
            jax.ShapeDtypeStruct((1, count), BF16),
        ),
        compiler_params=params(),
        name="combine",
        cost_estimate=cost(3),
    )(back.reshape(1, slots), slot, target_row)
    gradient = dot_nn(fixed_resid, fixed_rows)
    spread = jnp.broadcast_to(gradient[None], (devices, 1, FIX))
    gradients = lax.all_to_all(spread, ALL, split_axis=0, concat_axis=0, tiled=True)

    lower, inverses, done = factor_fixed(whole)
    gradients, done = lax.optimization_barrier((gradients, done))
    gradient = jnp.sum(gradients, axis=0) + done[:1, :1]
    count_blocks = NBLK * (NBLK + 1) // 2
    near = pl.BlockSpec(memory_space=pltpu.VMEM)
    fixed_coef, row_scores = pl.pallas_call(
        solve_kernel,
        out_shape=(
            jax.ShapeDtypeStruct((1, FIX), F32),
            jax.ShapeDtypeStruct((1, count), F32),
        ),
        in_specs=[pl.BlockSpec(memory_space=pl.ANY), near, near, near, near],
        out_specs=(near, near),
        scratch_shapes=[
            pltpu.VMEM((count_blocks, 64, 8, 128), F32),
            pltpu.SemaphoreType.DMA((count_blocks,)),
        ],
        compiler_params=params(48),
        name="substitute",
        cost_estimate=cost(12),
    )(lower, inverses, gradient, fixed_rows, member_score)
    return (fixed_coef.reshape(FIX), member_coef, row_scores.reshape(count))


def solution(mesh):
    grid = Mesh(mesh.devices.reshape(4, 4, 4, 2), ALL)
    placed = (P(ALL, None), P(ALL, None), P(ALL), P(), P(ALL))
    return jax.shard_map(
        shards,
        mesh=grid,
        in_specs=placed,
        out_specs=(P(), P(ALL, None), P(ALL)),
        check_vma=False,
    )
```

```python
import functools

import jax
import jax.numpy as jnp
from jax import lax
from jax.experimental import pallas as pl
from jax.experimental.pallas import tpu as pltpu
from jax.sharding import Mesh
from jax.sharding import PartitionSpec as P

F32 = jnp.float32
BF16 = jnp.bfloat16
HIGH = lax.Precision.HIGHEST
ALL = ("z", "x", "y", "core")
CHIPS = ("z", "x", "y")

MEM_DEV = 4
RIDGE_FIXED = 4.0
RIDGE_MEMBER = 1.0

FIX = 2048
MEM = 256
PAY = 384
BLK = 256
NBLK = FIX // BLK
CORE_PAIRS = 18


def pair_table():
    table = []
    for core in range(2):
        pairs = []
        for i in range(4 * core, 4 * core + 4):
            pairs += [(i, (i + k) % NBLK) for k in range(4)]
        pairs += [(0, 4), (1, 5)] if core == 0 else [(6, 2), (7, 3)]
        table.append(sorted((max(p), min(p)) for p in pairs))
    return table


def params(mb=56):
    return pltpu.CompilerParams(vmem_limit_bytes=mb << 20)


def dot_nn(a, b, precision=None):
    return lax.dot_general(a, b, (((1,), (0,)), ((), ())), precision=precision, preferred_element_type=F32)


def dot_nt(a, b, precision=None):
    return lax.dot_general(a, b, (((1,), (1,)), ((), ())), precision=precision, preferred_element_type=F32)


def dot_tn(a, b, precision=None):
    return lax.dot_general(a, b, (((0,), (0,)), ((), ())), precision=precision, preferred_element_type=F32)


def cost(us):
    return pl.CostEstimate(flops=int(us * 1e9), transcendentals=0, bytes_accessed=int(us * 2e6))


def split3(v):
    hi = v.astype(BF16)
    rest = v - hi.astype(F32)
    mid = rest.astype(BF16)
    low = (rest - mid.astype(F32)).astype(BF16)
    return hi, mid, low


def as_left(v, axis):
    h, m, l = split3(v)
    return jnp.concatenate([h, h, m, h, l, m], axis=axis)


def as_right(v, axis):
    h, m, l = split3(v)
    return jnp.concatenate([h, m, h, l, h, m], axis=axis)


def full_nn(a, b):
    return dot_nn(as_left(a, 1), as_right(b, 0))


def full_nt(a, b):
    return dot_nt(as_left(a, 1), as_right(b, 1))


def over_lanes(v, c):
    return jnp.broadcast_to(v[:, c : c + 1], v.shape)


def over_rows(v, i):
    return jnp.broadcast_to(v[i : i + 1, :], v.shape)


def factor128(blocks, aside=None):
    n = len(blocks)
    sub = lax.broadcasted_iota(jnp.int32, (8, 128), 0)
    lane = lax.broadcasted_iota(jnp.int32, (8, 128), 1)
    a = [[blk[8 * t : 8 * t + 8, :] for t in range(16)] for blk in blocks]
    e = [[(lane == sub + 8 * t).astype(F32) for t in range(16)] for _ in blocks]
    out = [[] for _ in blocks]
    b = [[over_lanes(a[p][0], k) for k in range(8)] for p in range(n)]
    for s in range(16):
        more = s < 15
        if aside is not None:
            aside(s)
        r = [a[p][s] for p in range(n)]
        f = [e[p][s] for p in range(n)]
        if more:
            r1 = [a[p][s + 1] for p in range(n)]
            f1 = [e[p][s + 1] for p in range(n)]
            q = [[over_lanes(r1[p], 8 * s + k) for k in range(8)] for p in range(n)]
            bn = [[over_lanes(r1[p], 8 * s + 8 + k) for k in range(8)] for p in range(n)]
        scale = [jnp.zeros((8, 128), F32) for _ in range(n)]
        for i in range(8):
            for p in range(n):
                inv = 1.0 / over_rows(b[p][i], i)
                scale[p] = jnp.where(sub == i, inv, scale[p])
                ri, fi = over_rows(r[p], i), over_rows(f[p], i)
                if i < 7:
                    m = jnp.where(sub > i, b[p][i] * inv, 0.0)
                    r[p] = r[p] - m * ri
                    f[p] = f[p] - m * fi
                bk = [None] * 8
                for k in range(i + 1, 8):
                    bk[k] = over_rows(b[p][k], i)
                    b[p][k] = b[p][k] - m * bk[k]
                if more:
                    mq = q[p][i] * inv
                    r1[p] = r1[p] - mq * ri
                    f1[p] = f1[p] - mq * fi
                    for k in range(i + 1, 8):
                        q[p][k] = q[p][k] - mq * bk[k]
                    for k in range(8):
                        bn[p][k] = bn[p][k] - mq * over_rows(q[p][i], k)
        for p in range(n):
            root = jnp.sqrt(scale[p])
            y, z = r[p] * root, f[p] * root
            out[p].append(z)
            if more:
                a[p][s + 1], e[p][s + 1] = r1[p], f1[p]
                b[p] = bn[p]
            if s < 14:
                both = jnp.concatenate([y, z], axis=1)
                u = dot_tn(as_left(y, 0), as_right(both, 0))
                for t in range(s + 2, 16):
                    a[p][t] = a[p][t] - u[8 * t : 8 * t + 8, :128]
                    e[p][t] = e[p][t] - u[8 * t : 8 * t + 8, 128:]
    return [jnp.concatenate(o, axis=0) for o in out]


def dispatch_kernel(cap, fix_ref, prev_ref, target_ref, id_ref, rows_ref, send_ref, slot_ref):
    count = rows_ref.shape[0]
    owners = send_ref.shape[0] // cap
    prior = dot_nt(prev_ref[...], fix_ref[...])
    resid = (target_ref[...] - prior).astype(BF16)
    ids = id_ref[...]
    owner = ids // MEM_DEV
    local = ids - owner * MEM_DEV
    hot = lax.broadcasted_iota(jnp.int32, (owners, count), 0) == owner
    before = (
        lax.broadcasted_iota(jnp.int32, (count, count), 0)
        < lax.broadcasted_iota(jnp.int32, (count, count), 1)
    ).astype(BF16)
    ahead = dot_nn(hot.astype(BF16), before)
    place = jnp.sum(jnp.where(hot, ahead, 0.0), axis=0, keepdims=True)
    slot = owner * cap + place.astype(jnp.int32)
    slot_ref[...] = slot
    kind = lax.broadcasted_iota(jnp.int32, (128, count), 0)
    meta = jnp.where(
        kind == 0,
        jnp.broadcast_to(resid.astype(F32), (128, count)),
        (kind == local + 1).astype(F32),
    ).astype(BF16)
    rows = rows_ref[...]

    def place_rows(c, carry):
        pick = (
            lax.broadcasted_iota(jnp.int32, (256, count), 0) + 256 * c == slot
        ).astype(BF16)
        at = pl.ds(pl.multiple_of(256 * c, 256), 256)
        send_ref[at, :MEM] = dot_nn(pick, rows).astype(BF16)
        send_ref[at, MEM:] = dot_nt(pick, meta).astype(BF16)
        return carry

    lax.fori_loop(0, owners * cap // 256, place_rows, 0)


def member_kernel(recv_ref, coef_ref, score_ref, turned_ref, gram_ref, rhs_ref):
    slots = recv_ref.shape[0]
    unit = (
        lax.broadcasted_iota(jnp.int32, (PAY, PAY), 0)
        == lax.broadcasted_iota(jnp.int32, (PAY, PAY), 1)
    ).astype(BF16)

    def turn(c, carry):
        at = pl.ds(pl.multiple_of(256 * c, 256), 256)
        turned_ref[:, at] = dot_nt(unit, recv_ref[at, :]).astype(BF16)
        return carry

    lax.fori_loop(0, slots // 256, turn, 0)
    rows = recv_ref[:, :MEM]
    hots = turned_ref[MEM + 1 : MEM + 1 + MEM_DEV, :]
    resid = turned_ref[MEM : MEM + 1, :]
    rhs_ref[...] = dot_nn(hots * resid, rows)
    ridge = jnp.where(
        lax.broadcasted_iota(jnp.int32, (MEM, MEM), 0)
        == lax.broadcasted_iota(jnp.int32, (MEM, MEM), 1),
        RIDGE_MEMBER,
        0.0,
    )
    for m in range(MEM_DEV):
        gram_ref[m] = dot_nn(turned_ref[:MEM, :] * hots[m : m + 1, :], rows) + ridge

    grams = [gram_ref[m] for m in range(MEM_DEV)]
    w0 = factor128([g[:128, :128] for g in grams])
    l10 = [full_nt(g[128:, :128], w) for g, w in zip(grams, w0)]
    w1 = factor128([g[128:, 128:] - full_nt(l, l) for g, l in zip(grams, l10)])
    for m in range(MEM_DEV):
        right = rhs_ref[m : m + 1, :]
        y0 = full_nt(right[:, :128], w0[m])
        y1 = full_nt(right[:, 128:] - full_nt(y0, l10[m]), w1[m])
        x1 = full_nn(y1, w1[m])
        x0 = full_nn(y0 - full_nn(x1, l10[m]), w0[m])
        coef_ref[m : m + 1, :] = jnp.concatenate([x0, x1], axis=1)
    low = coef_ref[...].astype(BF16)
    projected = dot_nn(low, turned_ref[:MEM, :])
    score_ref[...] = jnp.sum(projected * hots.astype(F32), axis=0, keepdims=True)


def combine_kernel(back_ref, slot_ref, target_ref, score_ref, resid_ref):
    slots, count = back_ref.shape[1], slot_ref.shape[1]
    parts = split3(back_ref[...])
    stack = jnp.concatenate([part.astype(F32) for part in parts] + [jnp.zeros((5, slots), F32)], axis=0).astype(BF16)
    slot = slot_ref[...]
    total = jnp.zeros((8, count), F32)
    for c in range(slots // 256):
        pick = (
            lax.broadcasted_iota(jnp.int32, (256, count), 0) + 256 * c == slot
        ).astype(BF16)
        total = total + dot_nn(stack[:, 256 * c : 256 * c + 256], pick)
    score = total[0:1] + (total[1:2] + total[2:3])
    score_ref[...] = score
    resid_ref[...] = (target_ref[...] - score).astype(BF16)


def gram_kernel(hi_ref, lo_ref, own_ref, other_ref, out_ref, turned_ref):
    rows = own_ref.shape[0]
    unit = (
        lax.broadcasted_iota(jnp.int32, (BLK, BLK), 0)
        == lax.broadcasted_iota(jnp.int32, (BLK, BLK), 1)
    ).astype(BF16)
    for part, ref in enumerate((own_ref, other_ref)):
        for i in range(NBLK):
            turned_ref[i, :, rows * part : rows * part + rows] = dot_nt(
                unit, ref[:, BLK * i : BLK * i + BLK]
            ).astype(BF16)

    def block(b, carry):
        left = turned_ref[hi_ref[b]]
        lanes = pl.ds(pl.multiple_of(lo_ref[b] * BLK, BLK), BLK)
        value = dot_nn(left[:, :rows], own_ref[:, lanes]) + dot_nn(left[:, rows:], other_ref[:, lanes])
        out_ref[:32, b] = value[:, :128].reshape(32, 8, 128)
        out_ref[32:, b] = value[:, 128:].reshape(32, 8, 128)
        return carry

    lax.fori_loop(0, CORE_PAIRS, block, 0)


def gram_blocks(own, other, hi, lo):
    rows = own.shape[0]
    return pl.pallas_call(
        gram_kernel,
        out_shape=jax.ShapeDtypeStruct((64, CORE_PAIRS, 8, 128), F32),
        in_specs=[pl.BlockSpec(memory_space=pltpu.SMEM)] * 2
        + [pl.BlockSpec(memory_space=pltpu.VMEM)] * 2,
        out_specs=pl.BlockSpec(memory_space=pltpu.VMEM),
        scratch_shapes=[pltpu.VMEM((NBLK, BLK, 2 * rows), BF16)],
        compiler_params=params(56),
        name="gram",
        cost_estimate=cost(10),
    )(hi, lo, own, other)


def place_of(i, j):
    return i * (i + 1) // 2 + j


def read_block(a_ref, at):
    flat = a_ref[at].reshape(2 * BLK, 128)
    return jnp.concatenate([flat[:BLK], flat[BLK:]], axis=1)


def write_block(a_ref, at, value):
    a_ref[at] = jnp.concatenate([value[:, :128], value[:, 128:]], axis=0).reshape(64, 8, 128)


WIDE = 32
SLIM = 16


def job_table():
    spare = NBLK * (NBLK + 1) // 2
    table = []
    for k in range(NBLK):
        jobs = []
        if k:
            jobs = [(i, j, place_of(i, j)) for i in range(k, NBLK) for j in range(k, i + 1)][1:]
        jobs += [(NBLK - 1, NBLK - 1, spare)] * (WIDE - len(jobs))
        table.append([entry for job in jobs for entry in job])
    return table


def factor_kernel(table_ref, gram_ref, a_ref, w_ref, done_ref, left_ref, right_ref, sems):
    copies = []
    for core, pairs in enumerate(pair_table()):
        for b, (i, j) in enumerate(pairs):
            at = place_of(i, j)
            copies.append(
                pltpu.make_async_copy(gram_ref.at[:, core, b], a_ref.at[at], sems.at[at])
            )
    first = pair_table()[0].index((0, 0))
    copies = [copies[first]] + copies[:first] + copies[first + 1 :]
    for copy in copies:
        copy.start()
    copies[0].wait()
    left_ref[NBLK - 1] = jnp.zeros((BLK, 6 * BLK), BF16)
    right_ref[NBLK - 1] = jnp.zeros((BLK, 6 * BLK), BF16)
    a_ref[NBLK * (NBLK + 1) // 2] = jnp.zeros((64, 8, 128), F32)
    ridge = jnp.where(
        lax.broadcasted_iota(jnp.int32, (128, 128), 0)
        == lax.broadcasted_iota(jnp.int32, (128, 128), 1),
        RIDGE_FIXED,
        0.0,
    )

    def trail(i, j, at):
        gain = dot_nt(left_ref[i], right_ref[j])
        flat = jnp.concatenate([gain[:, :128], gain[:, 128:]], axis=0)
        a_ref[at] = a_ref[at] - flat.reshape(64, 8, 128)

    def diagonal(k, every):
        def aside(first):
            def emit(s):
                if s % every == 0:
                    slot = 3 * (first + s // every)
                    trail(table_ref[k, slot], table_ref[k, slot + 1], table_ref[k, slot + 2])

            return emit

        diag = a_ref[place_of(k, k)].reshape(2 * BLK, 128)
        w00 = factor128([diag[:128] + ridge], aside(0))[0]
        l10 = full_nt(diag[128:256], w00)
        cross = full_nn(l10, w00)
        w11 = factor128([diag[384:] + ridge - full_nt(l10, l10)], aside(16 // every))[0]
        w_ref[k, :128, :128] = w00
        w_ref[k, :128, 128:] = jnp.zeros((128, 128), F32)
        w_ref[k, 128:, :128] = -full_nn(w11, cross)
        w_ref[k, 128:, 128:] = w11

    def step(k, carry):
        wide = (k == 1) | (k == 2)

        @pl.when(wide)
        def _():
            diagonal(k, 1)

        @pl.when(jnp.logical_not(wide))
        def _():
            diagonal(k, 2)

        @pl.when(k == 0)
        def _():
            for copy in copies[1:]:
                copy.wait()

        whole = as_right(w_ref[k], 1)

        def panel(i, carry):
            at = place_of(i, k)
            value = dot_nt(as_left(read_block(a_ref, at), 1), whole)
            write_block(a_ref, at, value)
            h, m, l = split3(value)
            left_ref[i] = jnp.concatenate([h, h, m, h, l, m], axis=1)
            right_ref[i] = jnp.concatenate([h, m, h, l, h, m], axis=1)
            return carry

        lax.fori_loop(k + 1, NBLK, panel, 0)

        @pl.when(k + 1 < NBLK)
        def _():
            trail(k + 1, k + 1, place_of(k + 1, k + 1))

        return carry

    lax.fori_loop(0, NBLK, step, 0)
    done_ref[...] = jnp.zeros((8, 128), F32)


def factor_fixed(gram):
    count = NBLK * (NBLK + 1) // 2
    return pl.pallas_call(
        factor_kernel,
        out_shape=(
            jax.ShapeDtypeStruct((count + 1, 64, 8, 128), F32),
            jax.ShapeDtypeStruct((NBLK, BLK, BLK), F32),
            jax.ShapeDtypeStruct((8, 128), F32),
        ),
        in_specs=[pl.BlockSpec(memory_space=pltpu.SMEM), pl.BlockSpec(memory_space=pl.ANY)],
        out_specs=(
            pl.BlockSpec(memory_space=pltpu.VMEM),
            pl.BlockSpec(memory_space=pltpu.VMEM),
            pl.BlockSpec(memory_space=pltpu.VMEM),
        ),
        scratch_shapes=[
            pltpu.VMEM((NBLK, BLK, 6 * BLK), BF16),
            pltpu.VMEM((NBLK, BLK, 6 * BLK), BF16),
            pltpu.SemaphoreType.DMA((count,)),
        ],
        compiler_params=params(46),
        name="factor_fixed",
        cost_estimate=cost(100),
    )(jnp.array(job_table(), jnp.int32), gram)


def halves(a_ref, at):
    flat = a_ref[at].reshape(2 * BLK, 128)
    return flat[:BLK], flat[BLK:]


def solve_kernel(low_ref, w_ref, grad_ref, far_ref, member_ref, coef_ref, score_ref, a_ref, fix_ref, sems, fix_sem):
    copies = {}
    for k in range(1, NBLK):
        for j in range(k):
            at = place_of(k, j)
            copies[k, j] = pltpu.make_async_copy(low_ref.at[at], a_ref.at[at], sems.at[at])
            copies[k, j].start()
    fix_copy = pltpu.make_async_copy(far_ref, fix_ref, fix_sem)
    fix_copy.start()
    turned = [w_ref[k].T for k in range(NBLK)]

    def times_row(left, right, row):
        return left * row[:, :128] + right * row[:, 128:]

    def as_column(spread):
        return jnp.sum(spread, axis=1, keepdims=True)

    forward = []
    for k in range(NBLK):
        part = grad_ref[:, BLK * k : BLK * k + BLK].T
        if k:
            total = jnp.zeros((BLK, 128), F32)
            for j in range(k):
                copies[k, j].wait()
                left, right = halves(a_ref, place_of(k, j))
                total = total + times_row(left, right, forward[j])
            part = part - as_column(total)
        forward.append(jnp.sum(turned[k] * part, axis=0, keepdims=True))
    backward = [None] * NBLK
    for k in range(NBLK - 1, -1, -1):
        part = forward[k]
        if k + 1 < NBLK:
            total = [jnp.zeros((8, 128), F32) for _ in range(2)]
            for i in range(k + 1, NBLK):
                for h, piece in enumerate(halves(a_ref, place_of(i, k))):
                    gain = (piece * backward[i]).reshape(BLK // 8, 8, 128)
                    total[h] = total[h] + jnp.sum(gain, axis=0)
            part = part - jnp.concatenate(
                [jnp.sum(total[h], axis=0, keepdims=True) for h in range(2)], axis=1
            )
        backward[k] = as_column(times_row(turned[k][:, :128], turned[k][:, 128:], part))
    coef = jnp.concatenate([jnp.broadcast_to(x, (BLK, 128)).T[:1] for x in backward], axis=1)
    coef_ref[...] = coef
    fix_copy.wait()
    score_ref[...] = dot_nt(coef.astype(BF16), fix_ref[...]) + member_ref[...]


def shards(fixed_rows, member_rows, target, fixed_prev, member_id):
    count = fixed_rows.shape[0]
    devices = lax.axis_size(ALL)
    cap = 3 * count // devices
    slots = devices * cap
    core = lax.axis_index("core")
    swap = [(0, 1), (1, 0)]
    other = lax.ppermute(fixed_rows, "core", swap)

    table = jnp.array(pair_table(), jnp.int32)[core]
    gram = gram_blocks(fixed_rows, other, table[:, 0], table[:, 1])
    target_row = target.reshape(1, count)
    gram, ids = lax.optimization_barrier((gram, member_id.reshape(1, count)))
    shares = lax.all_to_all(gram, CHIPS, split_axis=0, concat_axis=0, tiled=True)
    send, slot = pl.pallas_call(
        functools.partial(dispatch_kernel, cap),
        out_shape=(
            jax.ShapeDtypeStruct((slots, PAY), BF16),
            jax.ShapeDtypeStruct((1, count), jnp.int32),
        ),
        compiler_params=params(),
        name="dispatch",
        cost_estimate=cost(9),
    )(fixed_rows, fixed_prev.reshape(1, FIX), target_row, ids, member_rows)
    shares, send = lax.optimization_barrier((shares, send))
    recv = lax.all_to_all(send.reshape(devices, cap, PAY), ALL, split_axis=0, concat_axis=0, tiled=True)
    share = jnp.sum(shares, axis=0)
    whole = lax.all_gather(share, ALL, axis=0, tiled=False)
    whole = whole.reshape(devices // 2, 2, CORE_PAIRS, 8, 128)

    member_coef, slot_score = pl.pallas_call(
        member_kernel,
        out_shape=(
            jax.ShapeDtypeStruct((MEM_DEV, MEM), F32),
            jax.ShapeDtypeStruct((1, slots), F32),
        ),
        scratch_shapes=[
            pltpu.VMEM((PAY, slots), BF16),
            pltpu.VMEM((MEM_DEV, MEM, MEM), F32),
            pltpu.VMEM((MEM_DEV, MEM), F32),
        ],
        compiler_params=params(),
        name="members",
        cost_estimate=cost(30),
    )(recv.reshape(slots, PAY))
    back = lax.all_to_all(slot_score.reshape(devices, cap), ALL, split_axis=0, concat_axis=0, tiled=True)
    member_score, fixed_resid = pl.pallas_call(
        combine_kernel,
        out_shape=(
            jax.ShapeDtypeStruct((1, count), F32),
            jax.ShapeDtypeStruct((1, count), BF16),
        ),
        compiler_params=params(),
        name="combine",
        cost_estimate=cost(3),
    )(back.reshape(1, slots), slot, target_row)
    gradient = dot_nn(fixed_resid, fixed_rows)
    spread = jnp.broadcast_to(gradient[None], (devices, 1, FIX))
    gradients = lax.all_to_all(spread, ALL, split_axis=0, concat_axis=0, tiled=True)

    lower, inverses, done = factor_fixed(whole)
    gradients, done = lax.optimization_barrier((gradients, done))
    gradient = jnp.sum(gradients, axis=0) + done[:1, :1]
    count_blocks = NBLK * (NBLK + 1) // 2
    near = pl.BlockSpec(memory_space=pltpu.VMEM)
    fixed_coef, row_scores = pl.pallas_call(
        solve_kernel,
        out_shape=(
            jax.ShapeDtypeStruct((1, FIX), F32),
            jax.ShapeDtypeStruct((1, count), F32),
        ),
        in_specs=[pl.BlockSpec(memory_space=pl.ANY), near, near, pl.BlockSpec(memory_space=pl.ANY), near],
        out_specs=(near, near),
        scratch_shapes=[
            pltpu.VMEM((count_blocks, 64, 8, 128), F32),
            pltpu.VMEM((count, FIX), BF16),
            pltpu.SemaphoreType.DMA((count_blocks,)),
            pltpu.SemaphoreType.DMA,
        ],
        compiler_params=params(48),
        name="substitute",
        cost_estimate=cost(12),
    )(lower, inverses, gradient, fixed_rows, member_score)
    return (fixed_coef.reshape(FIX), member_coef, row_scores.reshape(count))


def solution(mesh):
    grid = Mesh(mesh.devices.reshape(4, 4, 4, 2), ALL)
    placed = (P(ALL, None), P(ALL, None), P(ALL), P(), P(ALL))
    return jax.shard_map(
        shards,
        mesh=grid,
        in_specs=placed,
        out_specs=(P(), P(ALL, None), P(ALL)),
        check_vma=False,
    )
```

```python
import functools

import jax
import jax.numpy as jnp
from jax import lax
from jax.experimental import pallas as pl
from jax.experimental.pallas import tpu as pltpu
from jax.sharding import Mesh
from jax.sharding import PartitionSpec as P

F32 = jnp.float32
BF16 = jnp.bfloat16
HIGH = lax.Precision.HIGHEST
ALL = ("z", "x", "y", "core")
CHIPS = ("z", "x", "y")

MEM_DEV = 4
RIDGE_FIXED = 4.0
RIDGE_MEMBER = 1.0

FIX = 2048
MEM = 256
PAY = 384
BLK = 256
NBLK = FIX // BLK
CORE_PAIRS = 18


def pair_table():
    table = []
    for core in range(2):
        pairs = []
        for i in range(4 * core, 4 * core + 4):
            pairs += [(i, (i + k) % NBLK) for k in range(4)]
        pairs += [(0, 4), (1, 5)] if core == 0 else [(6, 2), (7, 3)]
        table.append(sorted((max(p), min(p)) for p in pairs))
    return table


def params(mb=56):
    return pltpu.CompilerParams(vmem_limit_bytes=mb << 20)


def dot_nn(a, b, precision=None):
    return lax.dot_general(a, b, (((1,), (0,)), ((), ())), precision=precision, preferred_element_type=F32)


def dot_nt(a, b, precision=None):
    return lax.dot_general(a, b, (((1,), (1,)), ((), ())), precision=precision, preferred_element_type=F32)


def dot_tn(a, b, precision=None):
    return lax.dot_general(a, b, (((0,), (0,)), ((), ())), precision=precision, preferred_element_type=F32)


def cost(us):
    return pl.CostEstimate(flops=int(us * 1e9), transcendentals=0, bytes_accessed=int(us * 2e6))


def split3(v):
    hi = v.astype(BF16)
    rest = v - hi.astype(F32)
    mid = rest.astype(BF16)
    low = (rest - mid.astype(F32)).astype(BF16)
    return hi, mid, low


def as_left(v, axis):
    h, m, l = split3(v)
    return jnp.concatenate([h, h, m, h, l, m], axis=axis)


def as_right(v, axis):
    h, m, l = split3(v)
    return jnp.concatenate([h, m, h, l, h, m], axis=axis)


def full_nn(a, b):
    return dot_nn(as_left(a, 1), as_right(b, 0))


def full_nt(a, b):
    return dot_nt(as_left(a, 1), as_right(b, 1))


def over_lanes(v, c):
    return jnp.broadcast_to(v[:, c : c + 1], v.shape)


def over_rows(v, i):
    return jnp.broadcast_to(v[i : i + 1, :], v.shape)


def factor128(blocks, aside=None):
    n = len(blocks)
    sub = lax.broadcasted_iota(jnp.int32, (8, 128), 0)
    lane = lax.broadcasted_iota(jnp.int32, (8, 128), 1)
    a = [[blk[8 * t : 8 * t + 8, :] for t in range(16)] for blk in blocks]
    e = [[(lane == sub + 8 * t).astype(F32) for t in range(16)] for _ in blocks]
    out = [[] for _ in blocks]
    b = [[over_lanes(a[p][0], k) for k in range(8)] for p in range(n)]
    for s in range(16):
        more = s < 15
        if aside is not None:
            aside(s)
        r = [a[p][s] for p in range(n)]
        f = [e[p][s] for p in range(n)]
        if more:
            r1 = [a[p][s + 1] for p in range(n)]
            f1 = [e[p][s + 1] for p in range(n)]
            q = [[over_lanes(r1[p], 8 * s + k) for k in range(8)] for p in range(n)]
            bn = [[over_lanes(r1[p], 8 * s + 8 + k) for k in range(8)] for p in range(n)]
        scale = [jnp.zeros((8, 128), F32) for _ in range(n)]
        for i in range(8):
            for p in range(n):
                inv = 1.0 / over_rows(b[p][i], i)
                scale[p] = jnp.where(sub == i, inv, scale[p])
                ri, fi = over_rows(r[p], i), over_rows(f[p], i)
                if i < 7:
                    m = jnp.where(sub > i, b[p][i] * inv, 0.0)
                    r[p] = r[p] - m * ri
                    f[p] = f[p] - m * fi
                bk = [None] * 8
                for k in range(i + 1, 8):
                    bk[k] = over_rows(b[p][k], i)
                    b[p][k] = b[p][k] - m * bk[k]
                if more:
                    mq = q[p][i] * inv
                    r1[p] = r1[p] - mq * ri
                    f1[p] = f1[p] - mq * fi
                    for k in range(i + 1, 8):
                        q[p][k] = q[p][k] - mq * bk[k]
                    for k in range(8):
                        bn[p][k] = bn[p][k] - mq * over_rows(q[p][i], k)
        for p in range(n):
            root = jnp.sqrt(scale[p])
            y, z = r[p] * root, f[p] * root
            out[p].append(z)
            if more:
                a[p][s + 1], e[p][s + 1] = r1[p], f1[p]
                b[p] = bn[p]
            if s < 14:
                both = jnp.concatenate([y, z], axis=1)
                u = dot_tn(as_left(y, 0), as_right(both, 0))
                for t in range(s + 2, 16):
                    a[p][t] = a[p][t] - u[8 * t : 8 * t + 8, :128]
                    e[p][t] = e[p][t] - u[8 * t : 8 * t + 8, 128:]
    return [jnp.concatenate(o, axis=0) for o in out]


def dispatch_kernel(cap, fix_ref, prev_ref, target_ref, id_ref, rows_ref, send_ref, slot_ref):
    count = rows_ref.shape[0]
    owners = send_ref.shape[0] // cap
    prior = dot_nt(prev_ref[...], fix_ref[...])
    resid = (target_ref[...] - prior).astype(BF16)
    ids = id_ref[...]
    owner = ids // MEM_DEV
    local = ids - owner * MEM_DEV
    hot = lax.broadcasted_iota(jnp.int32, (owners, count), 0) == owner
    before = (
        lax.broadcasted_iota(jnp.int32, (count, count), 0)
        < lax.broadcasted_iota(jnp.int32, (count, count), 1)
    ).astype(BF16)
    ahead = dot_nn(hot.astype(BF16), before)
    place = jnp.sum(jnp.where(hot, ahead, 0.0), axis=0, keepdims=True)
    slot = owner * cap + place.astype(jnp.int32)
    slot_ref[...] = slot
    kind = lax.broadcasted_iota(jnp.int32, (128, count), 0)
    meta = jnp.where(
        kind == 0,
        jnp.broadcast_to(resid.astype(F32), (128, count)),
        (kind == local + 1).astype(F32),
    ).astype(BF16)
    rows = rows_ref[...]

    def place_rows(c, carry):
        pick = (
            lax.broadcasted_iota(jnp.int32, (256, count), 0) + 256 * c == slot
        ).astype(BF16)
        at = pl.ds(pl.multiple_of(256 * c, 256), 256)
        send_ref[at, :MEM] = dot_nn(pick, rows).astype(BF16)
        send_ref[at, MEM:] = dot_nt(pick, meta).astype(BF16)
        return carry

    lax.fori_loop(0, owners * cap // 256, place_rows, 0)


def member_kernel(recv_ref, coef_ref, score_ref, turned_ref, gram_ref, rhs_ref):
    slots = recv_ref.shape[0]
    unit = (
        lax.broadcasted_iota(jnp.int32, (PAY, PAY), 0)
        == lax.broadcasted_iota(jnp.int32, (PAY, PAY), 1)
    ).astype(BF16)
    for c in range(slots // 256):
        turned_ref[:, 256 * c : 256 * c + 256] = dot_nt(
            unit, recv_ref[256 * c : 256 * c + 256, :]
        ).astype(BF16)
    rows = recv_ref[:, :MEM]
    hots = turned_ref[MEM + 1 : MEM + 1 + MEM_DEV, :]
    resid = turned_ref[MEM : MEM + 1, :]
    rhs_ref[...] = dot_nn(hots * resid, rows)
    ridge = jnp.where(
        lax.broadcasted_iota(jnp.int32, (MEM, MEM), 0)
        == lax.broadcasted_iota(jnp.int32, (MEM, MEM), 1),
        RIDGE_MEMBER,
        0.0,
    )
    for m in range(MEM_DEV):
        gram_ref[m] = dot_nn(turned_ref[:MEM, :] * hots[m : m + 1, :], rows) + ridge

    grams = [gram_ref[m] for m in range(MEM_DEV)]
    w0 = factor128([g[:128, :128] for g in grams])
    l10 = [full_nt(g[128:, :128], w) for g, w in zip(grams, w0)]
    w1 = factor128([g[128:, 128:] - full_nt(l, l) for g, l in zip(grams, l10)])
    for m in range(MEM_DEV):
        right = rhs_ref[m : m + 1, :]
        y0 = full_nt(right[:, :128], w0[m])
        y1 = full_nt(right[:, 128:] - full_nt(y0, l10[m]), w1[m])
        x1 = full_nn(y1, w1[m])
        x0 = full_nn(y0 - full_nn(x1, l10[m]), w0[m])
        coef_ref[m : m + 1, :] = jnp.concatenate([x0, x1], axis=1)
    low = coef_ref[...].astype(BF16)
    projected = dot_nn(low, turned_ref[:MEM, :])
    score_ref[...] = jnp.sum(projected * hots.astype(F32), axis=0, keepdims=True)


def combine_kernel(back_ref, slot_ref, target_ref, score_ref, resid_ref):
    slots, count = back_ref.shape[1], slot_ref.shape[1]
    parts = split3(back_ref[...])
    stack = jnp.concatenate([part.astype(F32) for part in parts] + [jnp.zeros((5, slots), F32)], axis=0).astype(BF16)
    slot = slot_ref[...]
    total = jnp.zeros((8, count), F32)
    for c in range(slots // 256):
        pick = (
            lax.broadcasted_iota(jnp.int32, (256, count), 0) + 256 * c == slot
        ).astype(BF16)
        total = total + dot_nn(stack[:, 256 * c : 256 * c + 256], pick)
    score = total[0:1] + (total[1:2] + total[2:3])
    score_ref[...] = score
    resid_ref[...] = (target_ref[...] - score).astype(BF16)


def gram_kernel(hi_ref, lo_ref, own_ref, other_ref, out_ref, turned_ref):
    rows = own_ref.shape[0]
    unit = (
        lax.broadcasted_iota(jnp.int32, (BLK, BLK), 0)
        == lax.broadcasted_iota(jnp.int32, (BLK, BLK), 1)
    ).astype(BF16)
    for part, ref in enumerate((own_ref, other_ref)):
        for i in range(NBLK):
            turned_ref[i, :, rows * part : rows * part + rows] = dot_nt(
                unit, ref[:, BLK * i : BLK * i + BLK]
            ).astype(BF16)

    def block(b, carry):
        left = turned_ref[hi_ref[b]]
        lanes = pl.ds(pl.multiple_of(lo_ref[b] * BLK, BLK), BLK)
        value = dot_nn(left[:, :rows], own_ref[:, lanes]) + dot_nn(left[:, rows:], other_ref[:, lanes])
        out_ref[:32, b] = value[:, :128].reshape(32, 8, 128)
        out_ref[32:, b] = value[:, 128:].reshape(32, 8, 128)
        return carry

    lax.fori_loop(0, CORE_PAIRS, block, 0)


def gram_blocks(own, other, hi, lo):
    rows = own.shape[0]
    return pl.pallas_call(
        gram_kernel,
        out_shape=jax.ShapeDtypeStruct((64, CORE_PAIRS, 8, 128), F32),
        in_specs=[pl.BlockSpec(memory_space=pltpu.SMEM)] * 2
        + [pl.BlockSpec(memory_space=pltpu.VMEM)] * 2,
        out_specs=pl.BlockSpec(memory_space=pltpu.VMEM),
        scratch_shapes=[pltpu.VMEM((NBLK, BLK, 2 * rows), BF16)],
        compiler_params=params(56),
        name="gram",
        cost_estimate=cost(10),
    )(hi, lo, own, other)


def place_of(i, j):
    return i * (i + 1) // 2 + j


def read_block(a_ref, at):
    flat = a_ref[at].reshape(2 * BLK, 128)
    return jnp.concatenate([flat[:BLK], flat[BLK:]], axis=1)


def write_block(a_ref, at, value):
    a_ref[at] = jnp.concatenate([value[:, :128], value[:, 128:]], axis=0).reshape(64, 8, 128)


WIDE = 32
SLIM = 16


def job_table():
    spare = NBLK * (NBLK + 1) // 2
    table = []
    for k in range(NBLK):
        jobs = []
        if k:
            jobs = [(i, j, place_of(i, j)) for i in range(k, NBLK) for j in range(k, i + 1)][1:]
        jobs += [(NBLK - 1, NBLK - 1, spare)] * (WIDE - len(jobs))
        table.append([entry for job in jobs for entry in job])
    return table


def factor_kernel(table_ref, gram_ref, a_ref, w_ref, done_ref, left_ref, right_ref, sems):
    copies = []
    for core, pairs in enumerate(pair_table()):
        for b, (i, j) in enumerate(pairs):
            at = place_of(i, j)
            copies.append(
                pltpu.make_async_copy(gram_ref.at[:, core, b], a_ref.at[at], sems.at[at])
            )
    first = pair_table()[0].index((0, 0))
    copies = [copies[first]] + copies[:first] + copies[first + 1 :]
    for copy in copies:
        copy.start()
    copies[0].wait()
    left_ref[NBLK - 1] = jnp.zeros((BLK, 6 * BLK), BF16)
    right_ref[NBLK - 1] = jnp.zeros((BLK, 6 * BLK), BF16)
    a_ref[NBLK * (NBLK + 1) // 2] = jnp.zeros((64, 8, 128), F32)
    ridge = jnp.where(
        lax.broadcasted_iota(jnp.int32, (128, 128), 0)
        == lax.broadcasted_iota(jnp.int32, (128, 128), 1),
        RIDGE_FIXED,
        0.0,
    )

    def trail(i, j, at):
        gain = dot_nt(left_ref[i], right_ref[j])
        flat = jnp.concatenate([gain[:, :128], gain[:, 128:]], axis=0)
        a_ref[at] = a_ref[at] - flat.reshape(64, 8, 128)

    def diagonal(k, every):
        def aside(first):
            def emit(s):
                if s % every == 0:
                    slot = 3 * (first + s // every)
                    trail(table_ref[k, slot], table_ref[k, slot + 1], table_ref[k, slot + 2])

            return emit

        diag = a_ref[place_of(k, k)].reshape(2 * BLK, 128)
        w00 = factor128([diag[:128] + ridge], aside(0))[0]
        l10 = full_nt(diag[128:256], w00)
        cross = full_nn(l10, w00)
        w11 = factor128([diag[384:] + ridge - full_nt(l10, l10)], aside(16 // every))[0]
        w_ref[k, :128, :128] = w00
        w_ref[k, :128, 128:] = jnp.zeros((128, 128), F32)
        w_ref[k, 128:, :128] = -full_nn(w11, cross)
        w_ref[k, 128:, 128:] = w11

    def step(k, carry):
        wide = (k == 1) | (k == 2)

        @pl.when(wide)
        def _():
            diagonal(k, 1)

        @pl.when(jnp.logical_not(wide))
        def _():
            diagonal(k, 2)

        @pl.when(k == 0)
        def _():
            for copy in copies[1:]:
                copy.wait()

        whole = as_right(w_ref[k], 1)

        def panel(i, carry):
            at = place_of(i, k)
            value = dot_nt(as_left(read_block(a_ref, at), 1), whole)
            write_block(a_ref, at, value)
            h, m, l = split3(value)
            left_ref[i] = jnp.concatenate([h, h, m, h, l, m], axis=1)
            right_ref[i] = jnp.concatenate([h, m, h, l, h, m], axis=1)
            return carry

        lax.fori_loop(k + 1, NBLK, panel, 0)

        @pl.when(k + 1 < NBLK)
        def _():
            trail(k + 1, k + 1, place_of(k + 1, k + 1))

        return carry

    lax.fori_loop(0, NBLK, step, 0)
    done_ref[...] = jnp.zeros((8, 128), F32)


def factor_fixed(gram):
    count = NBLK * (NBLK + 1) // 2
    return pl.pallas_call(
        factor_kernel,
        out_shape=(
            jax.ShapeDtypeStruct((count + 1, 64, 8, 128), F32),
            jax.ShapeDtypeStruct((NBLK, BLK, BLK), F32),
            jax.ShapeDtypeStruct((8, 128), F32),
        ),
        in_specs=[pl.BlockSpec(memory_space=pltpu.SMEM), pl.BlockSpec(memory_space=pl.ANY)],
        out_specs=(
            pl.BlockSpec(memory_space=pltpu.VMEM),
            pl.BlockSpec(memory_space=pltpu.VMEM),
            pl.BlockSpec(memory_space=pltpu.VMEM),
        ),
        scratch_shapes=[
            pltpu.VMEM((NBLK, BLK, 6 * BLK), BF16),
            pltpu.VMEM((NBLK, BLK, 6 * BLK), BF16),
            pltpu.SemaphoreType.DMA((count,)),
        ],
        compiler_params=params(46),
        name="factor_fixed",
        cost_estimate=cost(100),
    )(jnp.array(job_table(), jnp.int32), gram)


def halves(a_ref, at):
    flat = a_ref[at].reshape(2 * BLK, 128)
    return flat[:BLK], flat[BLK:]


def solve_kernel(low_ref, w_ref, grad_ref, far_ref, member_ref, coef_ref, score_ref, a_ref, fix_ref, sems, fix_sem):
    copies = {}
    for k in range(1, NBLK):
        for j in range(k):
            at = place_of(k, j)
            copies[k, j] = pltpu.make_async_copy(low_ref.at[at], a_ref.at[at], sems.at[at])
            copies[k, j].start()
    fix_copy = pltpu.make_async_copy(far_ref, fix_ref, fix_sem)
    fix_copy.start()
    turned = [w_ref[k].T for k in range(NBLK)]

    def times_row(left, right, row):
        return left * row[:, :128] + right * row[:, 128:]

    def as_column(spread):
        return jnp.sum(spread, axis=1, keepdims=True)

    forward = []
    for k in range(NBLK):
        part = grad_ref[:, BLK * k : BLK * k + BLK].T
        if k:
            total = jnp.zeros((BLK, 128), F32)
            for j in range(k):
                copies[k, j].wait()
                left, right = halves(a_ref, place_of(k, j))
                total = total + times_row(left, right, forward[j])
            part = part - as_column(total)
        forward.append(jnp.sum(turned[k] * part, axis=0, keepdims=True))
    backward = [None] * NBLK
    for k in range(NBLK - 1, -1, -1):
        part = forward[k]
        if k + 1 < NBLK:
            total = [jnp.zeros((8, 128), F32) for _ in range(2)]
            for i in range(k + 1, NBLK):
                for h, piece in enumerate(halves(a_ref, place_of(i, k))):
                    gain = (piece * backward[i]).reshape(BLK // 8, 8, 128)
                    total[h] = total[h] + jnp.sum(gain, axis=0)
            part = part - jnp.concatenate(
                [jnp.sum(total[h], axis=0, keepdims=True) for h in range(2)], axis=1
            )
        backward[k] = as_column(times_row(turned[k][:, :128], turned[k][:, 128:], part))
    coef = jnp.concatenate([jnp.broadcast_to(x, (BLK, 128)).T[:1] for x in backward], axis=1)
    coef_ref[...] = coef
    fix_copy.wait()
    score_ref[...] = dot_nt(coef.astype(BF16), fix_ref[...]) + member_ref[...]


def shards(fixed_rows, member_rows, target, fixed_prev, member_id):
    count = fixed_rows.shape[0]
    devices = lax.axis_size(ALL)
    cap = 3 * count // devices
    slots = devices * cap
    core = lax.axis_index("core")
    swap = [(0, 1), (1, 0)]
    other = lax.ppermute(fixed_rows, "core", swap)

    table = jnp.array(pair_table(), jnp.int32)[core]
    gram = gram_blocks(fixed_rows, other, table[:, 0], table[:, 1])
    target_row = target.reshape(1, count)
    gram, ids = lax.optimization_barrier((gram, member_id.reshape(1, count)))
    shares = lax.all_to_all(gram, CHIPS, split_axis=0, concat_axis=0, tiled=True)
    send, slot = pl.pallas_call(
        functools.partial(dispatch_kernel, cap),
        out_shape=(
            jax.ShapeDtypeStruct((slots, PAY), BF16),
            jax.ShapeDtypeStruct((1, count), jnp.int32),
        ),
        compiler_params=params(),
        name="dispatch",
        cost_estimate=cost(9),
    )(fixed_rows, fixed_prev.reshape(1, FIX), target_row, ids, member_rows)
    shares, send = lax.optimization_barrier((shares, send))
    recv = lax.all_to_all(send.reshape(devices, cap, PAY), ALL, split_axis=0, concat_axis=0, tiled=True)
    share = jnp.sum(shares, axis=0)
    whole = lax.all_gather(share, ALL, axis=0, tiled=False)
    whole = whole.reshape(devices // 2, 2, CORE_PAIRS, 8, 128)

    member_coef, slot_score = pl.pallas_call(
        member_kernel,
        out_shape=(
            jax.ShapeDtypeStruct((MEM_DEV, MEM), F32),
            jax.ShapeDtypeStruct((1, slots), F32),
        ),
        scratch_shapes=[
            pltpu.VMEM((PAY, slots), BF16),
            pltpu.VMEM((MEM_DEV, MEM, MEM), F32),
            pltpu.VMEM((MEM_DEV, MEM), F32),
        ],
        compiler_params=params(),
        name="members",
        cost_estimate=cost(30),
    )(recv.reshape(slots, PAY))
    back = lax.all_to_all(slot_score.reshape(devices, cap), ALL, split_axis=0, concat_axis=0, tiled=True)
    member_score, fixed_resid = pl.pallas_call(
        combine_kernel,
        out_shape=(
            jax.ShapeDtypeStruct((1, count), F32),
            jax.ShapeDtypeStruct((1, count), BF16),
        ),
        compiler_params=params(),
        name="combine",
        cost_estimate=cost(3),
    )(back.reshape(1, slots), slot, target_row)
    gradient = dot_nn(fixed_resid, fixed_rows)
    spread = jnp.broadcast_to(gradient[None], (devices, 1, FIX))
    gradients = lax.all_to_all(spread, ALL, split_axis=0, concat_axis=0, tiled=True)

    lower, inverses, done = factor_fixed(whole)
    gradients, done = lax.optimization_barrier((gradients, done))
    gradient = jnp.sum(gradients, axis=0) + done[:1, :1]
    count_blocks = NBLK * (NBLK + 1) // 2
    near = pl.BlockSpec(memory_space=pltpu.VMEM)
    fixed_coef, row_scores = pl.pallas_call(
        solve_kernel,
        out_shape=(
            jax.ShapeDtypeStruct((1, FIX), F32),
            jax.ShapeDtypeStruct((1, count), F32),
        ),
        in_specs=[pl.BlockSpec(memory_space=pl.ANY), near, near, pl.BlockSpec(memory_space=pl.ANY), near],
        out_specs=(near, near),
        scratch_shapes=[
            pltpu.VMEM((count_blocks, 64, 8, 128), F32),
            pltpu.VMEM((count, FIX), BF16),
            pltpu.SemaphoreType.DMA((count_blocks,)),
            pltpu.SemaphoreType.DMA,
        ],
        compiler_params=params(48),
        name="substitute",
        cost_estimate=cost(12),
    )(lower, inverses, gradient, fixed_rows, member_score)
    return (fixed_coef.reshape(FIX), member_coef, row_scores.reshape(count))


def solution(mesh):
    grid = Mesh(mesh.devices.reshape(4, 4, 4, 2), ALL)
    placed = (P(ALL, None), P(ALL, None), P(ALL), P(), P(ALL))
    return jax.shard_map(
        shards,
        mesh=grid,
        in_specs=placed,
        out_specs=(P(), P(ALL, None), P(ALL)),
        check_vma=False,
    )
```
